512 devices in a mesh: gr: 32 (over y, x), gc: 16 (over z, core).
Axes of the slice: x: 4, y: 8, z: 8, core: 2. Of those that a mesh axis runs over, the one named last changes fastest.
Arguments:
- features: bfloat16 [16, 32, 512, 128], P('gc', 'gr'), may hold values from -6 to 6
- out_grad: bfloat16 [32, 16, 512, 128], P('gr', 'gc'), may hold values from -6 to 6
- weight: bfloat16 [128, 128], replicated, may hold values from -0.5 to 0.5
- block_values: bfloat16 [32, 16, 128, 128, 128], P('gr', 'gc'), may hold values from 0 to 0.03491211
- block_slot: int32 [32, 16, 128], P('gr', 'gc'), may hold values from 0 to 2047, as said below
- live_count: int32 [32, 16], P('gr', 'gc'), may hold values from 32 to 128, as said below
- row_need: int32 [32, 16, 16, 2], P('gr', 'gc'), may hold values from 0 to 3, as said below
- col_need: int32 [32, 16, 32, 2], P('gr', 'gc'), may hold values from 0 to 3, as said below
Outputs:
- activated: bfloat16 [32, 16, 512, 128], P('gr', 'gc')
- weight_grad: float32 [128, 128], replicated
- input_grad: bfloat16 [16, 32, 512, 128], P('gc', 'gr')
The draws below stay inside these ranges and needn't reach their ends.
Inputs may be any that keep to these rules, and one draw needn't show every extreme that they name: `block_slot`: within one tile the 128 entries are distinct. `live_count`: each tile holds 128, 64 or 32 live slots; some tile holds 128 in every draw. `row_need`: the 2 entries for one tile and one owner are distinct. `col_need`: the 2 entries for one tile and one owner are distinct.
All inputs are finite; a program needn't handle non-finite values.
Results may differ from the reference program's by a relative error of at most 0.0069.
Values may be sent and summed in bfloat16 or wider, within the bound.
No kernel may reach another device: no remote copies, remote signals or barrier semaphores. Data moves between devices by JAX's collectives and lax.ppermute only.
A program may use at most 64 MiB of HBM per device.

```python
import jax
import jax.numpy as jnp
from jax import lax

F = 128
BLK = 128
NL = 512
NZB = 128
CAP = 2
NODES = 262144
N_GR = 32
N_GC = 16


def distinct_pick(key, lead, total, keep):
    scores = jax.random.randint(key, lead + (total,), 0, 2 ** 30 // total) * total + jnp.arange(total)
    return jnp.argsort(scores, axis=-1)[..., :keep].astype(jnp.int32)


def draw_block_slot(key, part):
    slot_total = N_GC * CAP * N_GR * CAP
    return distinct_pick(jax.random.fold_in(key, 11), (N_GR, N_GC), slot_total, NZB)


def draw_row_need(key, part):
    return distinct_pick(jax.random.fold_in(key, 12), (N_GR, N_GC, N_GC), NL // BLK, CAP)


def draw_col_need(key, part):
    return distinct_pick(jax.random.fold_in(key, 13), (N_GR, N_GC, N_GR), NL // BLK, CAP)


def draw_live_count(key, part):
    levels = jax.random.randint(jax.random.fold_in(key, 14), (N_GR * N_GC,), 0, 3)
    divisor = jnp.where(levels == 0, 1, jnp.where(levels == 1, 2, 4))
    counts = NZB // divisor
    fullest = jax.random.randint(jax.random.fold_in(key, 15), (), 0, N_GR * N_GC)
    counts = jnp.where(jnp.arange(N_GR * N_GC) == fullest, NZB, counts)
    return counts.reshape(N_GR, N_GC).astype(jnp.int32)


def level_of(key, dims, cuts, low, top_value):
    loudness, own = 1.0, jax.random.fold_in(key, 6)
    for dim, parts in cuts:
        steps = jnp.exp(jax.random.uniform(jax.random.fold_in(own, dim), (parts,), jnp.float32, low / len(cuts), top_value / len(cuts)))
        loudness = loudness * jnp.repeat(steps, dims[dim] // parts).reshape([-1 if axis == dim else 1 for axis in range(len(dims))])
    return loudness


def scatter_about(key, shape, scale, reach, pieces=(), held_as=jnp.bfloat16):
    level = level_of(key, shape, pieces, -0.22, 0.18) if pieces else 1.0
    result = jax.random.normal(key, shape, jnp.float32) * scale * level
    return jnp.minimum(jnp.maximum(result, -reach), reach).astype(held_as)


def setup_inputs(seed: int = 0) -> dict:
    arg_keys = jax.random.split(jax.random.key(seed), 9)
    return {
        "features": scatter_about(arg_keys[0], (N_GC, N_GR, NL, F), 1.0, 6.0, ((0, 16), (1, 32))),
        "out_grad": scatter_about(arg_keys[1], (N_GR, N_GC, NL, F), 1.0, 6.0, ((0, 32), (1, 16))),
        "weight": scatter_about(arg_keys[2], (F, F), F ** -0.5, 0.5),
        "block_values": jnp.clip(0.03491211 * jax.random.uniform(arg_keys[3], (N_GR, N_GC, NZB, BLK, BLK), jnp.float32) ** level_of(arg_keys[3], (N_GR, N_GC, NZB, BLK, BLK), ((0, 32), (1, 16)), -0.2, 0.2), 0.0, 0.03491211).astype(jnp.bfloat16),
        "block_slot": draw_block_slot(jax.random.fold_in(arg_keys[8], 71), 0),
        "live_count": draw_live_count(jax.random.fold_in(arg_keys[8], 71), 0),
        "row_need": draw_row_need(jax.random.fold_in(arg_keys[8], 71), 0),
        "col_need": draw_col_need(jax.random.fold_in(arg_keys[8], 71), 0),
    }


def reference(features, out_grad, weight, block_values, block_slot, live_count, row_need, col_need):
    per_dev = NL // BLK
    col_slots = N_GR * CAP
    row_slots = N_GC * CAP
    feature_blocks = features.reshape(N_GC, N_GR, per_dev, BLK, F)

    def forward_tile(tile, accum):
        i = tile // N_GC
        j = tile % N_GC
        values = block_values[i, j].astype(jnp.float32)
        slots = block_slot[i, j]
        live = (jnp.arange(NZB) < live_count[i, j]).astype(jnp.float32)
        row_of = slots // col_slots
        col_of = slots % col_slots
        picked = feature_blocks[j][jnp.arange(N_GR)[:, None], col_need[i, j]]
        picked = picked.reshape(col_slots, BLK, F).astype(jnp.float32)
        terms = jnp.einsum("bmk,bkf->bmf", values, picked[col_of]) * live[:, None, None]
        partial_value = jax.ops.segment_sum(terms, row_of, num_segments=row_slots).astype(jnp.bfloat16)
        partial_value = lax.optimization_barrier(partial_value).astype(jnp.float32)
        owners = jnp.arange(row_slots) // CAP
        blocks = row_need[i, j].reshape(-1)
        return accum.at[i, owners, blocks].add(partial_value)

    start = jnp.zeros((N_GR, N_GC, per_dev, BLK, F), jnp.float32)
    accum = lax.fori_loop(0, N_GR * N_GC, forward_tile, start)
    aggregated = accum.astype(jnp.bfloat16).reshape(-1, F)
    pre = jnp.dot(aggregated, weight, preferred_element_type=jnp.float32)
    sig = jax.nn.sigmoid(pre)
    activated = (pre * sig).astype(jnp.bfloat16)
    upstream = out_grad.reshape(-1, F).astype(jnp.float32)
    grad_pre = (upstream * sig * (1.0 + pre * (1.0 - sig))).astype(jnp.bfloat16)
    weight_grad = jnp.dot(aggregated.T, grad_pre, preferred_element_type=jnp.float32) * (float(NODES) ** -0.5)
    back_rows = jnp.dot(grad_pre, weight.T, preferred_element_type=jnp.float32).astype(jnp.bfloat16)
    back_blocks = back_rows.reshape(N_GR, N_GC, per_dev, BLK, F)

    def backward_tile(tile, accum):
        i = tile // N_GC
        j = tile % N_GC
        values = block_values[i, j].astype(jnp.float32)
        slots = block_slot[i, j]
        live = (jnp.arange(NZB) < live_count[i, j]).astype(jnp.float32)
        row_of = slots // col_slots
        col_of = slots % col_slots
        picked = back_blocks[i][jnp.arange(N_GC)[:, None], row_need[i, j]]
        picked = picked.reshape(row_slots, BLK, F).astype(jnp.float32)
        terms = jnp.einsum("bmk,bmf->bkf", values, picked[row_of]) * live[:, None, None]
        partial_value = jax.ops.segment_sum(terms, col_of, num_segments=col_slots).astype(jnp.bfloat16)
        partial_value = lax.optimization_barrier(partial_value).astype(jnp.float32)
        sources = jnp.arange(col_slots) // CAP
        blocks = col_need[i, j].reshape(-1)
        return accum.at[j, sources, blocks].add(partial_value)

    start_back = jnp.zeros((N_GC, N_GR, per_dev, BLK, F), jnp.float32)
    accum_back = lax.fori_loop(0, N_GR * N_GC, backward_tile, start_back)
    input_grad = accum_back.astype(jnp.bfloat16).reshape(N_GC, N_GR, NL, F)
    return activated.reshape(N_GR, N_GC, NL, F), weight_grad, input_grad
```

```python
import jax
import jax.numpy as jnp
from jax import lax
from jax.experimental import pallas as pl
from jax.experimental.pallas import tpu as pltpu
from jax.sharding import PartitionSpec as P

F32 = jnp.float32
BF16 = jnp.bfloat16
EXTRA = 16
GROUP = 8

VMEM = pl.BlockSpec(memory_space=pltpu.VMEM)
SMEM = pl.BlockSpec(memory_space=pltpu.SMEM)


def call(kernel, out_shape, in_specs, scratch=(), flops=0, moved=0):
    many = isinstance(out_shape, (tuple, list))
    return pl.pallas_call(
        kernel,
        out_shape=out_shape,
        in_specs=in_specs,
        out_specs=tuple(VMEM for _ in out_shape) if many else VMEM,
        scratch_shapes=list(scratch),
        cost_estimate=pl.CostEstimate(flops=flops, bytes_accessed=moved, transcendentals=0),
        compiler_params=pltpu.CompilerParams(vmem_limit_bytes=48 * 1024 * 1024),
    )


def pick_kernel(asked, feats, out):
    n, _, _ = out.shape
    blk = out.shape[1] // 2

    def step(r, carry):
        for k in range(2):
            start = pl.multiple_of(asked[r, k] * blk, blk)
            out[r, k * blk : (k + 1) * blk, :] = feats[pl.ds(start, blk), :]
        return carry

    lax.fori_loop(0, n, step, 0, unroll=4)


def forward_kernel(col_slots, slots, live, row_need, values, arrived, out, acc):
    n, _, width = out.shape
    blk = values.shape[1]
    acc[...] = jnp.zeros_like(acc)

    def group(g, carry):
        for u in range(GROUP):
            b = g * GROUP + u
            slot = slots[0, b]
            row = slot // col_slots
            col = slot % col_slots
            feats = arrived[col // 2, pl.ds(pl.multiple_of((col % 2) * blk, blk), blk), :]
            acc[row] += jnp.dot(values[b], feats, preferred_element_type=F32)
        return carry

    lax.fori_loop(0, live[0, 0] // GROUP, group, 0)
    sub = lax.broadcasted_iota(jnp.int32, (EXTRA, width), 0)
    for c in range(n):
        for k in range(2):
            out[c, k * blk : (k + 1) * blk, :] = acc[2 * c + k].astype(BF16)
        ids = jnp.where(sub < EXTRA // 2, row_need[c, 0], row_need[c, 1])
        out[c, 2 * blk :, :] = ids.astype(F32).astype(BF16)


def middle_kernel(arrived, weight, upstream, act, out, agg, back):
    n, rows, width = arrived.shape
    blk = (rows - EXTRA) // 2
    per_dev = upstream.shape[0] // blk
    ids = []
    for c in range(n):
        tail = arrived[c, 2 * blk :, :].astype(F32)
        ids.append((tail[0:1, :], tail[EXTRA // 2 : EXTRA // 2 + 1, :]))
    w = weight[...]
    total = jnp.zeros((width, width), F32)
    for q in range(per_dev):
        acc = jnp.zeros((blk, width), F32)
        for c in range(n):
            for k in range(2):
                term = arrived[c, k * blk : (k + 1) * blk, :].astype(F32)
                acc = acc + jnp.where(ids[c][k] == float(q), term, 0.0)
        a = acc.astype(BF16)
        pre = jnp.dot(a, w, preferred_element_type=F32)
        sig = jax.nn.sigmoid(pre)
        act[q * blk : (q + 1) * blk, :] = (pre * sig).astype(BF16)
        up = upstream[q * blk : (q + 1) * blk, :].astype(F32)
        grad = (up * sig * (1.0 + pre * (1.0 - sig))).astype(BF16)
        total = total + lax.dot_general(a, grad, (((0,), (0,)), ((), ())), preferred_element_type=F32)
        back[q] = lax.dot_general(
            grad, w, (((1,), (1,)), ((), ())), preferred_element_type=F32
        ).astype(BF16)
    high = total.astype(BF16).astype(F32)
    low = total - high
    step = width // n
    for c in range(n):
        for k in range(2):
            chosen = back[0]
            for q in range(1, per_dev):
                chosen = jnp.where(ids[c][k].astype(BF16) == float(q), back[q], chosen)
            out[c, k * blk : (k + 1) * blk, :] = chosen
        pair = [high[c * step : (c + 1) * step, :], low[c * step : (c + 1) * step, :]]
        out[c, 2 * blk :, :] = jnp.concatenate(pair, axis=0).astype(BF16)


def backward_kernel(col_slots, slots, live, values, arrived, out, acc):
    blk = values.shape[1]
    acc[...] = jnp.zeros_like(acc)

    def group(g, carry):
        for u in range(GROUP):
            b = g * GROUP + u
            slot = slots[0, b]
            row = slot // col_slots
            col = slot % col_slots
            grads = arrived[row // 2, pl.ds(pl.multiple_of((row % 2) * blk, blk), blk), :]
            acc[col] += lax.dot_general(
                values[b], grads, (((0,), (0,)), ((), ())), preferred_element_type=F32
            )
        return carry

    lax.fori_loop(0, live[0, 0] // GROUP, group, 0)
    for r in range(out.shape[0]):
        for k in range(2):
            out[r, k * blk : (k + 1) * blk, :] = acc[2 * r + k].astype(BF16)


def final_kernel(asked, arrived, out, acc):
    n, rows, _ = arrived.shape
    blk = rows // 2
    acc[...] = jnp.zeros_like(acc)

    def step(r, carry):
        for k in range(2):
            term = arrived[r, k * blk : (k + 1) * blk, :].astype(F32)
            acc[asked[r, k]] += term
        return carry

    lax.fori_loop(0, n, step, 0, unroll=2)
    for q in range(acc.shape[0]):
        out[q * blk : (q + 1) * blk, :] = acc[q].astype(BF16)


def on_device(features, out_grad, weight, block_values, block_slot, live_count, row_need, col_need):
    import functools

    n_rows = lax.axis_size("gr")
    n_cols = lax.axis_size("gc")
    values = block_values[0, 0]
    slot_total, blk, _ = values.shape
    local, width = features.shape[2:]
    cap = row_need.shape[3]
    per_dev = local // blk
    col_slots = n_rows * cap
    row_slots = n_cols * cap
    slots = block_slot[0]
    step = width // n_cols
    work = 2 * slot_total * blk * blk * width

    need = jnp.pad(col_need[0, 0], ((0, 0), (0, 128 - cap))).reshape(n_rows, 1, 128)
    asked = lax.all_to_all(need, "gr", split_axis=0, concat_axis=0, tiled=True)
    asked = asked.reshape(n_rows, 128)
    chosen = call(
        pick_kernel,
        jax.ShapeDtypeStruct((n_rows, cap * blk, width), BF16),
        [SMEM, VMEM],
        moved=4 << 20,
    )(asked, features[0, 0])
    arrived = lax.all_to_all(chosen, "gr", split_axis=0, concat_axis=0, tiled=True)
    partial = call(
        functools.partial(forward_kernel, col_slots),
        jax.ShapeDtypeStruct((n_cols, cap * blk + EXTRA, width), BF16),
        [SMEM, SMEM, SMEM, VMEM, VMEM],
        [pltpu.VMEM((row_slots, blk, width), F32)],
        flops=work,
        moved=8 << 20,
    )(slots, live_count, row_need[0, 0], values, arrived)
    partial = lax.all_to_all(partial, "gc", split_axis=0, concat_axis=0, tiled=True)
    activated, back = call(
        middle_kernel,
        (
            jax.ShapeDtypeStruct((local, width), BF16),
            jax.ShapeDtypeStruct((n_cols, cap * blk + EXTRA, width), BF16),
        ),
        [VMEM, VMEM, VMEM],
        [pltpu.VMEM((per_dev, blk, width), BF16), pltpu.VMEM((per_dev, blk, width), BF16)],
        flops=work // 8,
        moved=4 << 20,
    )(partial, weight, out_grad[0, 0])
    back = lax.all_to_all(back, "gc", split_axis=0, concat_axis=0, tiled=True)
    tail = back[:, cap * blk :, :].astype(F32).sum(0)
    tail = tail[:step] + tail[step:]
    tail = jnp.broadcast_to(tail[None], (n_rows, step, width))
    tail = lax.all_to_all(tail, "gr", split_axis=0, concat_axis=0, tiled=True).sum(0)
    tail = jnp.broadcast_to(tail[None], (n_cols, step, width))
    tail = lax.all_to_all(tail, "gc", split_axis=0, concat_axis=0, tiled=True)
    node_total = local * n_rows * n_cols
    weight_grad = tail.reshape(width, width) * float(node_total) ** (-0.5)
    returned = call(
        functools.partial(backward_kernel, col_slots),
        jax.ShapeDtypeStruct((n_rows, cap * blk, width), BF16),
        [SMEM, SMEM, VMEM, VMEM],
        [pltpu.VMEM((col_slots, blk, width), F32)],
        flops=work,
        moved=8 << 20,
    )(slots, live_count, values, back)
    returned = lax.all_to_all(returned, "gr", split_axis=0, concat_axis=0, tiled=True)
    input_grad = call(
        final_kernel,
        jax.ShapeDtypeStruct((local, width), BF16),
        [SMEM, VMEM],
        [pltpu.VMEM((per_dev, blk, width), F32)],
        moved=4 << 20,
    )(asked, returned)
    return (
        activated.reshape(1, 1, local, width),
        weight_grad,
        input_grad.reshape(1, 1, local, width),
    )


def solution(mesh):
    placed = (
        P("gc", "gr", None, None),
        P("gr", "gc", None, None),
        P(),
        P("gr", "gc", None, None, None),
        P("gr", "gc", None),
        P("gr", "gc"),
        P("gr", "gc", None, None),
        P("gr", "gc", None, None),
    )
    return jax.shard_map(
        on_device,
        mesh=mesh,
        in_specs=placed,
        out_specs=(P("gr", "gc", None, None), P(), P("gc", "gr", None, None)),
        check_vma=False,
    )
```

```python
import functools

import jax
import jax.numpy as jnp
from jax import lax
from jax.experimental import pallas as pl
from jax.experimental.pallas import tpu as pltpu
from jax.sharding import PartitionSpec as P

F32 = jnp.float32
BF16 = jnp.bfloat16
EXTRA = 16
GROUP = 8
BATCH = 2

VMEM = pl.BlockSpec(memory_space=pltpu.VMEM)
SMEM = pl.BlockSpec(memory_space=pltpu.SMEM)
HBM = pl.BlockSpec(memory_space=pltpu.HBM)


def call(kernel, out_shape, in_specs, scratch=(), flops=0, moved=0, out_spec=VMEM, grant=48):
    many = isinstance(out_shape, (tuple, list))
    return pl.pallas_call(
        kernel,
        out_shape=out_shape,
        in_specs=in_specs,
        out_specs=tuple(out_spec for _ in out_shape) if many else out_spec,
        scratch_shapes=list(scratch),
        cost_estimate=pl.CostEstimate(flops=flops, bytes_accessed=moved, transcendentals=0),
        compiler_params=pltpu.CompilerParams(vmem_limit_bytes=grant << 20),
    )


def pick_kernel(asked, feats, out, sems):
    n = out.shape[0]
    blk = out.shape[1] // 2

    def copy(r, k):
        start = pl.multiple_of(asked[r, k] * blk, blk)
        return pltpu.make_async_copy(
            feats.at[pl.ds(start, blk), :], out.at[r, pl.ds(k * blk, blk), :], sems.at[r, k]
        )

    for r in range(n):
        for k in range(2):
            copy(r, k).start()
    for r in range(n):
        for k in range(2):
            copy(r, k).wait()


def load_groups(live, source, values, sems):
    groups = live[0, 0] // GROUP

    def load(g):
        part = pl.ds(pl.multiple_of(g * GROUP, GROUP), GROUP)
        return pltpu.make_async_copy(source.at[part], values.at[part], sems.at[g])

    def start(g, carry):
        load(g).start()
        return carry

    lax.fori_loop(0, groups, start, 0)
    return groups, load


def forward_kernel(
    col_slots, slots, live, row_need, source, arrived, out, values, acc, sems
):
    n, _, width = out.shape
    blk = values.shape[1]
    groups, load = load_groups(live, source, values, sems)
    acc[...] = jnp.zeros_like(acc)

    def group(g, carry):
        load(g).wait()
        for first in range(0, GROUP, BATCH):
            terms = []
            for u in range(first, first + BATCH):
                b = g * GROUP + u
                slot = slots[0, b]
                col = slot % col_slots
                feats = arrived[col // 2, pl.ds(pl.multiple_of((col % 2) * blk, blk), blk), :]
                term = jnp.dot(values[b], feats, preferred_element_type=F32)
                terms.append((slot // col_slots, term))
            for row, term in terms:
                acc[row] += term
        return carry

    lax.fori_loop(0, groups, group, 0)
    sub = lax.broadcasted_iota(jnp.int32, (EXTRA, width), 0)
    for c in range(n):
        for k in range(2):
            out[c, k * blk : (k + 1) * blk, :] = acc[2 * c + k].astype(BF16)
        ids = jnp.where(sub < EXTRA // 2, row_need[c, 0], row_need[c, 1])
        out[c, 2 * blk :, :] = ids.astype(F32).astype(BF16)


def middle_kernel(arrived, weight, upstream, act, out, local_term, back):
    n, rows, width = arrived.shape
    blk = (rows - EXTRA) // 2
    per_dev = upstream.shape[0] // blk
    ids = []
    for c in range(n):
        tail = arrived[c, 2 * blk :, :].astype(F32)
        ids.append((tail[0:1, :], tail[EXTRA // 2 : EXTRA // 2 + 1, :]))
    w = weight[...]
    total = jnp.zeros((width, width), F32)
    for q in range(per_dev):
        acc = jnp.zeros((blk, width), F32)
        for c in range(n):
            for k in range(2):
                term = arrived[c, k * blk : (k + 1) * blk, :].astype(F32)
                acc = acc + jnp.where(ids[c][k] == float(q), term, 0.0)
        a = acc.astype(BF16)
        pre = jnp.dot(a, w, preferred_element_type=F32)
        sig = jax.nn.sigmoid(pre)
        act[q * blk : (q + 1) * blk, :] = (pre * sig).astype(BF16)
        up = upstream[q * blk : (q + 1) * blk, :].astype(F32)
        grad = (up * sig * (1.0 + pre * (1.0 - sig))).astype(BF16)
        total = total + lax.dot_general(a, grad, (((0,), (0,)), ((), ())), preferred_element_type=F32)
        back[q] = lax.dot_general(
            grad, w, (((1,), (1,)), ((), ())), preferred_element_type=F32
        ).astype(BF16)
    local_term[...] = total
    for c in range(n):
        for k in range(2):
            chosen = back[0]
            for q in range(1, per_dev):
                chosen = jnp.where(ids[c][k].astype(BF16) == float(q), back[q], chosen)
            out[c, k * blk : (k + 1) * blk, :] = chosen


def backward_kernel(
    col_slots, slots, live, source, arrived, out, values, acc, held, load_sems, sems
):
    blk = values.shape[1]
    groups, load = load_groups(live, source, values, load_sems)
    acc[...] = jnp.zeros_like(acc)

    def group(g, carry):
        load(g).wait()
        for first in range(0, GROUP, BATCH):
            terms = []
            for u in range(first, first + BATCH):
                b = g * GROUP + u
                slot = slots[0, b]
                row = slot // col_slots
                grads = arrived[row // 2, pl.ds(pl.multiple_of((row % 2) * blk, blk), blk), :]
                term = lax.dot_general(
                    values[b], grads, (((0,), (0,)), ((), ())), preferred_element_type=F32
                )
                terms.append((slot % col_slots, term))
            for col, term in terms:
                acc[col] += term
        return carry

    lax.fori_loop(0, groups, group, 0)
    n = out.shape[0]

    def copy(r):
        return pltpu.make_async_copy(held.at[r], out.at[r], sems.at[r])

    for r in range(n):
        for k in range(2):
            held[r, k * blk : (k + 1) * blk, :] = acc[2 * r + k].astype(BF16)
        if r:
            copy(r - 1).start()
    copy(n - 1).start()
    for r in range(n):
        copy(r).wait()


def final_kernel(asked, arrived, out, acc):
    n, rows, _ = arrived.shape
    blk = rows // 2
    acc[...] = jnp.zeros_like(acc)

    def step(r, carry):
        for k in range(2):
            term = arrived[r, k * blk : (k + 1) * blk, :].astype(F32)
            acc[asked[r, k]] += term
        return carry

    lax.fori_loop(0, n, step, 0, unroll=2)
    for q in range(acc.shape[0]):
        out[q * blk : (q + 1) * blk, :] = acc[q].astype(BF16)


def on_device(features, out_grad, weight, block_values, block_slot, live_count, row_need, col_need):
    n_rows = lax.axis_size("gr")
    n_cols = lax.axis_size("gc")
    values = block_values[0, 0]
    slot_total, blk, _ = values.shape
    local, width = features.shape[2:]
    cap = row_need.shape[3]
    per_dev = local // blk
    col_slots = n_rows * cap
    row_slots = n_cols * cap
    slots = block_slot[0]
    work = 2 * slot_total * blk * blk * width

    def swap(array, axis):
        return lax.all_to_all(array, axis, split_axis=0, concat_axis=0, tiled=True)

    def trade(array, axis, bit):
        pairs = [(i, i ^ bit) for i in range(lax.axis_size(axis))]
        return lax.ppermute(array, axis, pairs)

    def upper(axis, bit):
        return (lax.axis_index(axis) & bit) != 0

    need = jnp.pad(col_need[0, 0], ((0, 0), (0, 128 - cap))).reshape(n_rows, 1, 128)
    asked = swap(need, "gr").reshape(n_rows, 128)
    chosen = call(
        pick_kernel,
        jax.ShapeDtypeStruct((n_rows, cap * blk, width), BF16),
        [SMEM, VMEM],
        [pltpu.SemaphoreType.DMA((n_rows, cap))],
        moved=4 << 20,
        out_spec=HBM,
        grant=60,
    )(asked, features[0, 0])
    arrived = swap(chosen, "gr")
    partial = call(
        functools.partial(forward_kernel, col_slots),
        jax.ShapeDtypeStruct((n_cols, cap * blk + EXTRA, width), BF16),
        [SMEM, SMEM, SMEM, HBM, VMEM],
        [
            pltpu.VMEM(values.shape, BF16),
            pltpu.VMEM((row_slots, blk, width), F32),
            pltpu.SemaphoreType.DMA((slot_total // GROUP,)),
        ],
        flops=work,
        moved=8 << 20,
    )(slots, live_count, row_need[0, 0], values, arrived)
    partial = swap(partial, "gc")
    activated, back, term = call(
        middle_kernel,
        (
            jax.ShapeDtypeStruct((local, width), BF16),
            jax.ShapeDtypeStruct((n_cols, cap * blk, width), BF16),
            jax.ShapeDtypeStruct((width, width), F32),
        ),
        [VMEM, VMEM, VMEM],
        [pltpu.VMEM((per_dev, blk, width), BF16)],
        flops=work // 8,
        moved=4 << 20,
    )(partial, weight, out_grad[0, 0])
    back = swap(back, "gc")

    halved = []
    bit = 1
    while bit < n_rows:
        if len(halved) < 2:
            low, high = jnp.split(term, 2, axis=0)
            top = upper("gr", bit)
            term = jnp.where(top, high, low) + trade(jnp.where(top, low, high), "gr", bit)
            halved.append(bit)
        else:
            other = trade(term, "gr", bit)
            term = term + other
        bit *= 2
    bit = 1
    while bit < n_cols:
        term = term + trade(term, "gc", bit)
        bit *= 2
    for bit in reversed(halved):
        other = trade(term, "gr", bit)
        top = upper("gr", bit)
        term = jnp.concatenate([jnp.where(top, other, term), jnp.where(top, term, other)], axis=0)
    node_total = local * n_rows * n_cols
    weight_grad = term * float(node_total) ** (-0.5)

    returned = call(
        functools.partial(backward_kernel, col_slots),
        jax.ShapeDtypeStruct((n_rows, cap * blk, width), BF16),
        [SMEM, SMEM, HBM, VMEM],
        [
            pltpu.VMEM(values.shape, BF16),
            pltpu.VMEM((col_slots, blk, width), F32),
            pltpu.VMEM((n_rows, cap * blk, width), BF16),
            pltpu.SemaphoreType.DMA((slot_total // GROUP,)),
            pltpu.SemaphoreType.DMA((n_rows,)),
        ],
        flops=work,
        moved=8 << 20,
        out_spec=HBM,
        grant=59,
    )(slots, live_count, values, back)
    returned = swap(returned, "gr")
    input_grad = call(
        final_kernel,
        jax.ShapeDtypeStruct((local, width), BF16),
        [SMEM, VMEM],
        [pltpu.VMEM((per_dev, blk, width), F32)],
        moved=4 << 20,
    )(asked, returned)
    return (
        activated.reshape(1, 1, local, width),
        weight_grad,
        input_grad.reshape(1, 1, local, width),
    )


def solution(mesh):
    placed = (
        P("gc", "gr", None, None),
        P("gr", "gc", None, None),
        P(),
        P("gr", "gc", None, None, None),
        P("gr", "gc", None),
        P("gr", "gc"),
        P("gr", "gc", None, None),
        P("gr", "gc", None, None),
    )

    return jax.shard_map(
        on_device,
        mesh=mesh,
        in_specs=placed,
        out_specs=(P("gr", "gc", None, None), P(), P("gc", "gr", None, None)),
        check_vma=False,
    )
```

```python
import functools

import jax
import jax.numpy as jnp
from jax import lax
from jax.experimental import pallas as pl
from jax.experimental.pallas import tpu as pltpu
from jax.sharding import PartitionSpec as P

F32 = jnp.float32
BF16 = jnp.bfloat16
EXTRA = 16
NX = 4
GROUP = 8
BATCH = 2
PICK_GRANT = 40
BACKWARD_GRANT = 58
FORWARD_GRANT = 40

ANY = pl.BlockSpec(memory_space=pl.ANY)
VMEM = pl.BlockSpec(memory_space=pltpu.VMEM)
SMEM = pl.BlockSpec(memory_space=pltpu.SMEM)
HBM = pl.BlockSpec(memory_space=pltpu.HBM)


def call(kernel, out_shape, in_specs, scratch=(), flops=0, moved=0, out_spec=VMEM, grant=48):
    many = isinstance(out_shape, (tuple, list))
    return pl.pallas_call(
        kernel,
        out_shape=out_shape,
        in_specs=in_specs,
        out_specs=tuple(out_spec for _ in out_shape) if many else out_spec,
        scratch_shapes=list(scratch),
        cost_estimate=pl.CostEstimate(flops=flops, bytes_accessed=moved, transcendentals=0),
        compiler_params=pltpu.CompilerParams(vmem_limit_bytes=grant << 20),
    )


def pick_kernel(me, *refs):
    peers = NX - 1
    tables, column, outs, sems = refs[:peers], refs[peers], refs[peers + 1 : -1], refs[-1]
    n = column.shape[0]
    blk = outs[0].shape[1] // 2
    mine = me[0, 0] % NX

    def copy(d, y, k):
        start = pl.multiple_of(tables[d][0, 2 * (NX * y + mine) + k] * blk, blk)
        return pltpu.make_async_copy(
            column.at[y, pl.ds(start, blk), :],
            outs[d].at[y, pl.ds(k * blk, blk), :],
            sems.at[d, y, k],
        )

    every = [(d, y, k) for d in range(peers) for y in range(n) for k in range(2)]
    for place in every:
        copy(*place).start()
    for place in every:
        copy(*place).wait()


def load_groups(live, source, values, sems):
    groups = live[0, 0] // GROUP

    def load(g):
        part = pl.ds(pl.multiple_of(g * GROUP, GROUP), GROUP)
        return pltpu.make_async_copy(source.at[part], values.at[part], sems.at[g])

    def start(g, carry):
        load(g).start()
        return carry

    lax.fori_loop(0, groups, start, 0)
    return groups, load


def forward_kernel(col_slots, me, slots, live, row_need, need, source, column, *refs):
    peers, (out, values, arrived, acc, sems, own_sems, peer_sems) = refs[: NX - 1], refs[NX - 1 :]
    n, _, width = out.shape
    blk = values.shape[1]
    rows = column.shape[0]
    mine = me[0, 0] % NX

    def own(y, k):
        start = pl.multiple_of(need[0, 2 * (NX * y + mine) + k] * blk, blk)
        return pltpu.make_async_copy(
            column.at[y, pl.ds(start, blk), :], arrived.at[0, 2 * y + k], own_sems.at[y, k]
        )

    def received(d):
        return pltpu.make_async_copy(peers[d], arrived.at[d + 1], peer_sems.at[d])

    every = [(y, k) for y in range(rows) for k in range(2)]
    for d in range(NX - 1):
        received(d).start()
    for place in every:
        own(*place).start()
    groups, load = load_groups(live, source, values, sems)
    acc[...] = jnp.zeros_like(acc)
    for d in range(NX - 1):
        received(d).wait()
    for place in every:
        own(*place).wait()

    def group(g, carry):
        load(g).wait()
        for first in range(0, GROUP, BATCH):
            terms = []
            for u in range(first, first + BATCH):
                b = g * GROUP + u
                slot = slots[0, b]
                col = slot % col_slots
                owner = col // 2
                piece = (mine + NX - owner % NX) % NX
                feats = arrived[piece, 2 * (owner // NX) + col % 2]
                term = jnp.dot(values[b], feats, preferred_element_type=F32)
                terms.append((slot // col_slots, term))
            for row, term in terms:
                acc[row] += term
        return carry

    lax.fori_loop(0, groups, group, 0)
    sub = lax.broadcasted_iota(jnp.int32, (EXTRA, width), 0)
    for c in range(n):
        for k in range(2):
            out[c, k * blk : (k + 1) * blk, :] = acc[2 * c + k].astype(BF16)
        ids = jnp.where(sub < EXTRA // 2, row_need[c, 0], row_need[c, 1])
        out[c, 2 * blk :, :] = ids.astype(F32).astype(BF16)


def middle_kernel(arrived, weight, upstream, act, out, local_term, back):
    n, rows, width = arrived.shape
    blk = (rows - EXTRA) // 2
    per_dev = upstream.shape[0] // blk
    ids = []
    for c in range(n):
        tail = arrived[c, 2 * blk :, :].astype(F32)
        ids.append((tail[0:1, :], tail[EXTRA // 2 : EXTRA // 2 + 1, :]))
    w = weight[...]
    total = jnp.zeros((width, width), F32)
    for q in range(per_dev):
        acc = jnp.zeros((blk, width), F32)
        for c in range(n):
            for k in range(2):
                term = arrived[c, k * blk : (k + 1) * blk, :].astype(F32)
                acc = acc + jnp.where(ids[c][k] == float(q), term, 0.0)
        a = acc.astype(BF16)
        pre = jnp.dot(a, w, preferred_element_type=F32)
        sig = jax.nn.sigmoid(pre)
        act[q * blk : (q + 1) * blk, :] = (pre * sig).astype(BF16)
        up = upstream[q * blk : (q + 1) * blk, :].astype(F32)
        grad = (up * sig * (1.0 + pre * (1.0 - sig))).astype(BF16)
        total = total + lax.dot_general(a, grad, (((0,), (0,)), ((), ())), preferred_element_type=F32)
        back[q] = lax.dot_general(
            grad, w, (((1,), (1,)), ((), ())), preferred_element_type=F32
        ).astype(BF16)
    local_term[...] = total
    for c in range(n):
        for k in range(2):
            chosen = back[0]
            for q in range(1, per_dev):
                chosen = jnp.where(ids[c][k].astype(BF16) == float(q), back[q], chosen)
            out[c, k * blk : (k + 1) * blk, :] = chosen


def backward_kernel(
    col_slots, slots, live, source, arrived, out, values, acc, held, load_sems, sems
):
    blk = values.shape[1]
    groups, load = load_groups(live, source, values, load_sems)
    acc[...] = jnp.zeros_like(acc)

    def group(g, carry):
        load(g).wait()
        for first in range(0, GROUP, BATCH):
            terms = []
            for u in range(first, first + BATCH):
                b = g * GROUP + u
                slot = slots[0, b]
                row = slot // col_slots
                grads = arrived[row // 2, pl.ds(pl.multiple_of((row % 2) * blk, blk), blk), :]
                term = lax.dot_general(
                    values[b], grads, (((0,), (0,)), ((), ())), preferred_element_type=F32
                )
                terms.append((slot % col_slots, term))
            for col, term in terms:
                acc[col] += term
        return carry

    lax.fori_loop(0, groups, group, 0)
    n = out.shape[0]

    def copy(r):
        return pltpu.make_async_copy(held.at[r], out.at[r], sems.at[r])

    for r in range(n):
        for k in range(2):
            held[r, k * blk : (k + 1) * blk, :] = acc[2 * r + k].astype(BF16)
        if r:
            copy(r - 1).start()
    copy(n - 1).start()
    for r in range(n):
        copy(r).wait()


def final_kernel(me, asked, arrived, out, acc):
    n, rows, _ = arrived.shape
    blk = rows // 2
    mine = me[0, 0]
    acc[...] = jnp.zeros_like(acc)

    def step(r, carry):
        ring = (r % NX + NX - mine % NX) % NX
        place = ((r // NX) ^ (mine // NX)) * NX + ring
        for k in range(2):
            term = arrived[r, k * blk : (k + 1) * blk, :].astype(F32)
            acc[asked[place, 2 * mine + k]] += term
        return carry

    lax.fori_loop(0, n, step, 0, unroll=2)
    for q in range(acc.shape[0]):
        out[q * blk : (q + 1) * blk, :] = acc[q].astype(BF16)


def on_device(features, out_grad, weight, block_values, block_slot, live_count, row_need, col_need):
    n_rows = lax.axis_size("gr")
    n_cols = lax.axis_size("gc")
    values = block_values[0, 0]
    slot_total, blk, _ = values.shape
    local, width = features.shape[2:]
    cap = row_need.shape[3]
    per_dev = local // blk
    col_slots = n_rows * cap
    row_slots = n_cols * cap
    slots = block_slot[0]
    work = 2 * slot_total * blk * blk * width

    def swap(array, axis):
        return lax.all_to_all(array, axis, split_axis=0, concat_axis=0, tiled=True)

    def trade(array, axis, bit):
        pairs = [(i, i ^ bit) for i in range(lax.axis_size(axis))]
        return lax.ppermute(array, axis, pairs)

    def upper(axis, bit):
        return (lax.axis_index(axis) & bit) != 0

    n_y = n_rows // NX
    me = lax.axis_index("gr").astype(jnp.int32).reshape(1, 1)

    def along_x(array, shift):
        pairs = [(i, i - i % NX + (i + shift) % NX) for i in range(n_rows)]
        return lax.ppermute(array, "gr", pairs)

    column = lax.all_to_all(
        jnp.broadcast_to(features[0, 0][None], (n_y, local, width)),
        "gr",
        split_axis=0,
        concat_axis=0,
        tiled=True,
        axis_index_groups=[[NX * y + x for y in range(n_y)] for x in range(NX)],
    )
    need = jnp.pad(col_need[0, 0].reshape(1, -1), ((0, 0), (0, 128 - col_slots)))
    tables = [along_x(need, -d) for d in range(1, NX)]
    chosen = call(
        pick_kernel,
        [jax.ShapeDtypeStruct((n_y, cap * blk, width), BF16) for _ in tables],
        [SMEM, *[SMEM for _ in tables], VMEM],
        [pltpu.SemaphoreType.DMA((NX - 1, n_y, cap))],
        moved=4 << 20,
        out_spec=ANY,
        grant=PICK_GRANT,
    )(me, *tables, column)
    pieces = [along_x(chosen[d], d + 1) for d in range(NX - 1)]
    pieces = [p.reshape(cap * n_y, blk, width) for p in pieces]
    partial = call(
        functools.partial(forward_kernel, col_slots),
        jax.ShapeDtypeStruct((n_cols, cap * blk + EXTRA, width), BF16),
        [SMEM, SMEM, SMEM, SMEM, SMEM, HBM, ANY, *[ANY for _ in pieces]],
        [
            pltpu.VMEM(values.shape, BF16),
            pltpu.VMEM((NX, cap * n_y, blk, width), BF16),
            pltpu.VMEM((row_slots, blk, width), F32),
            pltpu.SemaphoreType.DMA((slot_total // GROUP,)),
            pltpu.SemaphoreType.DMA((n_y, cap)),
            pltpu.SemaphoreType.DMA((NX - 1,)),
        ],
        flops=work,
        moved=8 << 20,
        grant=FORWARD_GRANT,
    )(me, slots, live_count, row_need[0, 0], need, values, column, *pieces)
    asked = jnp.concatenate([need, *tables], axis=0)
    bit = 1
    while bit < n_y:
        other = trade(asked, "gr", bit * NX)
        asked = jnp.concatenate([asked, other], axis=0)
        bit *= 2
    partial = swap(partial, "gc")
    activated, back, term = call(
        middle_kernel,
        (
            jax.ShapeDtypeStruct((local, width), BF16),
            jax.ShapeDtypeStruct((n_cols, cap * blk, width), BF16),
            jax.ShapeDtypeStruct((width, width), F32),
        ),
        [VMEM, VMEM, VMEM],
        [pltpu.VMEM((per_dev, blk, width), BF16)],
        flops=work // 8,
        moved=4 << 20,
    )(partial, weight, out_grad[0, 0])
    back = swap(back, "gc")

    halved = []
    bit = 1
    while bit < n_rows:
        if len(halved) < 2:
            low, high = jnp.split(term, 2, axis=0)
            top = upper("gr", bit)
            term = jnp.where(top, high, low) + trade(jnp.where(top, low, high), "gr", bit)
            halved.append(bit)
        else:
            other = trade(term, "gr", bit)
            term = term + other
        bit *= 2
    bit = 1
    while bit < n_cols:
        term = term + trade(term, "gc", bit)
        bit *= 2
    for bit in reversed(halved):
        other = trade(term, "gr", bit)
        top = upper("gr", bit)
        term = jnp.concatenate([jnp.where(top, other, term), jnp.where(top, term, other)], axis=0)
    node_total = local * n_rows * n_cols
    weight_grad = term * float(node_total) ** (-0.5)

    returned = call(
        functools.partial(backward_kernel, col_slots),
        jax.ShapeDtypeStruct((n_rows, cap * blk, width), BF16),
        [SMEM, SMEM, HBM, VMEM],
        [
            pltpu.VMEM(values.shape, BF16),
            pltpu.VMEM((col_slots, blk, width), F32),
            pltpu.VMEM((n_rows, cap * blk, width), BF16),
            pltpu.SemaphoreType.DMA((slot_total // GROUP,)),
            pltpu.SemaphoreType.DMA((n_rows,)),
        ],
        flops=work,
        moved=8 << 20,
        out_spec=HBM,
        grant=BACKWARD_GRANT,
    )(slots, live_count, values, back)
    returned = swap(returned, "gr")
    input_grad = call(
        final_kernel,
        jax.ShapeDtypeStruct((local, width), BF16),
        [SMEM, SMEM, VMEM],
        [pltpu.VMEM((per_dev, blk, width), F32)],
        moved=4 << 20,
    )(me, asked, returned)
    return (
        activated.reshape(1, 1, local, width),
        weight_grad,
        input_grad.reshape(1, 1, local, width),
    )


def solution(mesh):
    placed = (
        P("gc", "gr", None, None),
        P("gr", "gc", None, None),
        P(),
        P("gr", "gc", None, None, None),
        P("gr", "gc", None),
        P("gr", "gc"),
        P("gr", "gc", None, None),
        P("gr", "gc", None, None),
    )

    return jax.shard_map(
        on_device,
        mesh=mesh,
        in_specs=placed,
        out_specs=(P("gr", "gc", None, None), P(), P("gc", "gr", None, None)),
        check_vma=False,
    )
```

```python
import functools

import jax
import jax.numpy as jnp
from jax import lax
from jax.experimental import pallas as pl
from jax.experimental.pallas import tpu as pltpu
from jax.sharding import PartitionSpec as P

F32 = jnp.float32
BF16 = jnp.bfloat16
EXTRA = 16
NX = 4
GROUP = 8
BATCH = 2
PICK_GRANT = 40
BACKWARD_GRANT = 40
FORWARD_GRANT = 40

VMEM = pl.BlockSpec(memory_space=pltpu.VMEM)
SMEM = pl.BlockSpec(memory_space=pltpu.SMEM)
HBM = pl.BlockSpec(memory_space=pltpu.HBM)


def call(kernel, out_shape, in_specs, scratch=(), flops=0, moved=0, out_spec=VMEM, grant=48):
    many = isinstance(out_shape, (tuple, list))
    chosen = isinstance(out_spec, tuple)
    return pl.pallas_call(
        kernel,
        out_shape=out_shape,
        in_specs=in_specs,
        out_specs=(out_spec,) * len(out_shape) if many and not chosen else out_spec,
        scratch_shapes=list(scratch),
        cost_estimate=pl.CostEstimate(flops=flops, bytes_accessed=moved, transcendentals=0),
        compiler_params=pltpu.CompilerParams(vmem_limit_bytes=grant << 20),
    )


def repeat_kernel(feats, out, sems):
    n = out.shape[0]
    copies = [pltpu.make_async_copy(feats, out.at[y], sems.at[y]) for y in range(n)]
    for copy in copies:
        copy.start()
    for copy in copies:
        copy.wait()


def pick_kernel(me, *refs):
    peers = NX - 1
    tables, column, outs = refs[:peers], refs[peers], refs[peers + 1 :]
    blk = outs[0].shape[1] // 2
    mine = me[0, 0] & (NX - 1)

    def step(y, carry):
        for d in range(peers):
            for k in range(2):
                start = pl.multiple_of(tables[d][0, 2 * (NX * y + mine) + k] * blk, blk)
                outs[d][y, k * blk : (k + 1) * blk, :] = column[y, pl.ds(start, blk), :]
        return carry

    lax.fori_loop(0, column.shape[0], step, 0)


def shipper(held, out, sems):
    n = out.shape[0]

    def copy(c):
        return pltpu.make_async_copy(held.at[c], out.at[c], sems.at[c])

    def ship(c):
        if c:
            copy(c - 1).start()
        if c == n - 1:
            copy(c).start()
            for done in range(n):
                copy(done).wait()

    return ship


def load_groups(live, source, values, sems):
    groups = live[0, 0] >> 3

    def load(g):
        part = pl.ds(pl.multiple_of(g * GROUP, GROUP), GROUP)
        return pltpu.make_async_copy(source.at[part], values.at[part], sems.at[g])

    def start(g, carry):
        load(g).start()
        return carry

    lax.fori_loop(0, groups, start, 0)
    return groups, load


def forward_kernel(col_slots, me, slots, live, row_need, need, source, column, *refs):
    peers, (out, values, arrived, acc, held, sems, out_sems) = refs[: NX - 1], refs[NX - 1 :]
    n, _, width = out.shape
    blk = values.shape[1]
    mine = me[0, 0] & (NX - 1)
    shift = col_slots.bit_length() - 1
    groups, load = load_groups(live, source, values, sems)
    acc[...] = jnp.zeros_like(acc)

    def place(y, carry):
        for k in range(2):
            start = pl.multiple_of(need[0, 2 * (NX * y + mine) + k] * blk, blk)
            arrived[0, 2 * y + k] = column[y, pl.ds(start, blk), :]
            for d in range(NX - 1):
                arrived[d + 1, 2 * y + k] = peers[d][2 * y + k]
        return carry

    lax.fori_loop(0, column.shape[0], place, 0)

    def group(g, carry):
        load(g).wait()
        for first in range(0, GROUP, BATCH):
            terms = []
            for u in range(first, first + BATCH):
                b = g * GROUP + u
                slot = slots[0, b]
                col = slot & (col_slots - 1)
                piece = (mine - (col >> 1)) & (NX - 1)
                feats = arrived[piece, ((col >> 3) << 1) + (col & 1)]
                term = jnp.dot(values[b], feats, preferred_element_type=F32)
                terms.append((slot >> shift, term))
            for row, term in terms:
                acc[row] += term
        return carry

    lax.fori_loop(0, groups, group, 0)
    sub = lax.broadcasted_iota(jnp.int32, (EXTRA, width), 0)
    ship = shipper(held, out, out_sems)
    for c in range(n):
        for k in range(2):
            held[c, k * blk : (k + 1) * blk, :] = acc[2 * c + k].astype(BF16)
        ids = jnp.where(sub < EXTRA // 2, row_need[c, 0], row_need[c, 1])
        held[c, 2 * blk :, :] = ids.astype(F32).astype(BF16)
        ship(c)


def middle_kernel(
    arrived, weight, upstream, act, out, local_term, back, held, sems
):
    n, rows, width = arrived.shape
    blk = (rows - EXTRA) // 2
    per_dev = upstream.shape[0] // blk
    ids = []
    for c in range(n):
        tail = arrived[c, 2 * blk :, :].astype(F32)
        ids.append((tail[0:1, :], tail[EXTRA // 2 : EXTRA // 2 + 1, :]))
    w = weight[...]
    total = jnp.zeros((width, width), F32)
    for q in range(per_dev):
        acc = jnp.zeros((blk, width), F32)
        for c in range(n):
            for k in range(2):
                term = arrived[c, k * blk : (k + 1) * blk, :].astype(F32)
                acc = acc + jnp.where(ids[c][k] == float(q), term, 0.0)
        a = acc.astype(BF16)
        pre = jnp.dot(a, w, preferred_element_type=F32)
        sig = jax.nn.sigmoid(pre)
        act[q * blk : (q + 1) * blk, :] = (pre * sig).astype(BF16)
        up = upstream[q * blk : (q + 1) * blk, :].astype(F32)
        grad = (up * sig * (1.0 + pre * (1.0 - sig))).astype(BF16)
        total = total + lax.dot_general(a, grad, (((0,), (0,)), ((), ())), preferred_element_type=F32)
        back[q] = lax.dot_general(
            grad, w, (((1,), (1,)), ((), ())), preferred_element_type=F32
        ).astype(BF16)
    local_term[...] = total
    ship = shipper(held, out, sems)
    for c in range(n):
        for k in range(2):
            chosen = back[0]
            for q in range(1, per_dev):
                chosen = jnp.where(ids[c][k].astype(BF16) == float(q), back[q], chosen)
            held[c, k * blk : (k + 1) * blk, :] = chosen
        ship(c)


def backward_kernel(
    col_slots, slots, live, source, arrived, out, values, acc, held, load_sems, sems
):
    blk = values.shape[1]
    shift = col_slots.bit_length() - 1
    groups, load = load_groups(live, source, values, load_sems)
    acc[...] = jnp.zeros_like(acc)

    def group(g, carry):
        load(g).wait()
        for first in range(0, GROUP, BATCH):
            terms = []
            for u in range(first, first + BATCH):
                b = g * GROUP + u
                slot = slots[0, b]
                grads = arrived[slot >> shift]
                term = lax.dot_general(
                    values[b], grads, (((0,), (0,)), ((), ())), preferred_element_type=F32
                )
                terms.append((slot & (col_slots - 1), term))
            for col, term in terms:
                acc[col] += term
        return carry

    lax.fori_loop(0, groups, group, 0)
    ship = shipper(held, out, sems)
    for r in range(out.shape[0]):
        for k in range(2):
            held[r, k * blk : (k + 1) * blk, :] = acc[2 * r + k].astype(BF16)
        ship(r)


def final_kernel(me, asked, arrived, out, acc):
    n, rows, _ = arrived.shape
    blk = rows // 2
    mine = me[0, 0]
    acc[...] = jnp.zeros_like(acc)

    def step(r, carry):
        ring = (r - mine) & (NX - 1)
        place = ((r ^ mine) & ~(NX - 1)) | ring
        for k in range(2):
            term = arrived[r, k * blk : (k + 1) * blk, :].astype(F32)
            acc[asked[place, 2 * mine + k]] += term
        return carry

    lax.fori_loop(0, n, step, 0, unroll=2)
    for q in range(acc.shape[0]):
        out[q * blk : (q + 1) * blk, :] = acc[q].astype(BF16)


def on_device(features, out_grad, weight, block_values, block_slot, live_count, row_need, col_need):
    n_rows = lax.axis_size("gr")
    n_cols = lax.axis_size("gc")
    values = pltpu.with_memory_space_constraint(block_values[0, 0], pltpu.HBM)
    slot_total, blk, _ = values.shape
    local, width = features.shape[2:]
    cap = row_need.shape[3]
    per_dev = local // blk
    col_slots = n_rows * cap
    row_slots = n_cols * cap
    slots = block_slot[0]
    work = 2 * slot_total * blk * blk * width

    def swap(array, axis):
        return lax.all_to_all(array, axis, split_axis=0, concat_axis=0, tiled=True)

    def trade(array, axis, bit):
        pairs = [(i, i ^ bit) for i in range(lax.axis_size(axis))]
        return lax.ppermute(array, axis, pairs)

    def upper(axis, bit):
        return (lax.axis_index(axis) & bit) != 0

    n_y = n_rows // NX
    me = lax.axis_index("gr").astype(jnp.int32).reshape(1, 1)

    def along_x(array, shift):
        pairs = [(i, i - i % NX + (i + shift) % NX) for i in range(n_rows)]
        return lax.ppermute(array, "gr", pairs)

    copies = call(
        repeat_kernel,
        jax.ShapeDtypeStruct((n_y, local, width), BF16),
        [VMEM],
        [pltpu.SemaphoreType.DMA((n_y,))],
        moved=2 << 20,
        out_spec=HBM,
        grant=60,
    )(features[0, 0])
    column = lax.all_to_all(
        copies,
        "gr",
        split_axis=0,
        concat_axis=0,
        tiled=True,
        axis_index_groups=[[NX * y + x for y in range(n_y)] for x in range(NX)],
    )
    need = jnp.pad(col_need[0, 0].reshape(1, -1), ((0, 0), (0, 128 - col_slots)))
    tables = [along_x(need, -d) for d in range(1, NX)]
    chosen = call(
        pick_kernel,
        [jax.ShapeDtypeStruct((n_y, cap * blk, width), BF16) for _ in tables],
        [SMEM, *[SMEM for _ in tables], VMEM],
        moved=4 << 20,
        grant=PICK_GRANT,
    )(me, *tables, column)
    pieces = [along_x(chosen[d], d + 1) for d in range(NX - 1)]
    pieces = [p.reshape(cap * n_y, blk, width) for p in pieces]
    partial = call(
        functools.partial(forward_kernel, col_slots),
        pltpu.HBM((n_cols, cap * blk + EXTRA, width), BF16),
        [SMEM, SMEM, SMEM, SMEM, SMEM, HBM, VMEM, *[VMEM for _ in pieces]],
        [
            pltpu.VMEM(values.shape, BF16),
            pltpu.VMEM((NX, cap * n_y, blk, width), BF16),
            pltpu.VMEM((row_slots, blk, width), F32),
            pltpu.VMEM((n_cols, cap * blk + EXTRA, width), BF16),
            pltpu.SemaphoreType.DMA((slot_total // GROUP,)),
            pltpu.SemaphoreType.DMA((n_cols,)),
        ],
        flops=work,
        moved=8 << 20,
        out_spec=HBM,
        grant=FORWARD_GRANT,
    )(me, slots, live_count, row_need[0, 0], need, values, column, *pieces)
    asked = jnp.concatenate([need, *tables], axis=0)
    bit = 1
    while bit < n_y:
        other = trade(asked, "gr", bit * NX)
        asked = jnp.concatenate([asked, other], axis=0)
        bit *= 2
    partial = swap(partial, "gc")
    activated, back, term = call(
        middle_kernel,
        (
            jax.ShapeDtypeStruct((local, width), BF16),
            pltpu.HBM((n_cols, cap * blk, width), BF16),
            jax.ShapeDtypeStruct((width, width), F32),
        ),
        [VMEM, VMEM, VMEM],
        [
            pltpu.VMEM((per_dev, blk, width), BF16),
            pltpu.VMEM((n_cols, cap * blk, width), BF16),
            pltpu.SemaphoreType.DMA((n_cols,)),
        ],
        out_spec=(VMEM, HBM, VMEM),
        flops=work // 8,
        moved=4 << 20,
    )(partial, weight, out_grad[0, 0])
    back = swap(back, "gc")

    halved = []
    bit = 1
    while bit < n_rows:
        if len(halved) < 2:
            low, high = jnp.split(term, 2, axis=0)
            top = upper("gr", bit)
            term = jnp.where(top, high, low) + trade(jnp.where(top, low, high), "gr", bit)
            halved.append(bit)
        else:
            other = trade(term, "gr", bit)
            term = term + other
        bit *= 2
    bit = 1
    while bit < n_cols:
        term = term + trade(term, "gc", bit)
        bit *= 2
    for bit in reversed(halved):
        other = trade(term, "gr", bit)
        top = upper("gr", bit)
        term = jnp.concatenate([jnp.where(top, other, term), jnp.where(top, term, other)], axis=0)
    node_total = local * n_rows * n_cols
    weight_grad = term * float(node_total) ** (-0.5)

    returned = call(
        functools.partial(backward_kernel, col_slots),
        pltpu.HBM((n_rows, cap * blk, width), BF16),
        [SMEM, SMEM, HBM, VMEM],
        [
            pltpu.VMEM(values.shape, BF16),
            pltpu.VMEM((col_slots, blk, width), F32),
            pltpu.VMEM((n_rows, cap * blk, width), BF16),
            pltpu.SemaphoreType.DMA((slot_total // GROUP,)),
            pltpu.SemaphoreType.DMA((n_rows,)),
        ],
        flops=work,
        moved=8 << 20,
        out_spec=HBM,
        grant=BACKWARD_GRANT,
    )(slots, live_count, values, back.reshape(row_slots, blk, width))
    returned = swap(returned, "gr")
    input_grad = call(
        final_kernel,
        jax.ShapeDtypeStruct((local, width), BF16),
        [SMEM, SMEM, VMEM],
        [pltpu.VMEM((per_dev, blk, width), F32)],
        moved=4 << 20,
    )(me, asked, returned)
    return (
        activated.reshape(1, 1, local, width),
        weight_grad,
        input_grad.reshape(1, 1, local, width),
    )


def solution(mesh):
    placed = (
        P("gc", "gr", None, None),
        P("gr", "gc", None, None),
        P(),
        P("gr", "gc", None, None, None),
        P("gr", "gc", None),
        P("gr", "gc"),
        P("gr", "gc", None, None),
        P("gr", "gc", None, None),
    )

    return jax.shard_map(
        on_device,
        mesh=mesh,
        in_specs=placed,
        out_specs=(P("gr", "gc", None, None), P(), P("gc", "gr", None, None)),
        check_vma=False,
    )
```

```python
import functools

import jax
import jax.numpy as jnp
from jax import lax
from jax.experimental import pallas as pl
from jax.experimental.pallas import tpu as pltpu
from jax.sharding import PartitionSpec as P

F32 = jnp.float32
BF16 = jnp.bfloat16
EXTRA = 16
NX = 4
GROUP = 8
BATCH = 2
PARTS = 4
ROWS = 32
PICK_GRANT = 40
BACKWARD_GRANT = 40
FORWARD_GRANT = 40

VMEM = pl.BlockSpec(memory_space=pltpu.VMEM)
SMEM = pl.BlockSpec(memory_space=pltpu.SMEM)
HBM = pl.BlockSpec(memory_space=pltpu.HBM)


def call(kernel, out_shape, in_specs, scratch=(), flops=0, moved=0, out_spec=VMEM, grant=48):
    many = isinstance(out_shape, (tuple, list))
    return pl.pallas_call(
        kernel,
        out_shape=out_shape,
        in_specs=in_specs,
        out_specs=(out_spec,) * len(out_shape) if many else out_spec,
        scratch_shapes=list(scratch),
        cost_estimate=pl.CostEstimate(flops=flops, bytes_accessed=moved, transcendentals=0),
        compiler_params=pltpu.CompilerParams(vmem_limit_bytes=grant << 20),
    )


def repeat_kernel(feats, out, sems):
    n = out.shape[0]
    copies = [pltpu.make_async_copy(feats, out.at[y], sems.at[y]) for y in range(n)]
    for copy in copies:
        copy.start()
    for copy in copies:
        copy.wait()


def pick_kernel(me, *refs):
    peers = NX - 1
    tables, column, outs = refs[:peers], refs[peers], refs[peers + 1 :]
    blk = outs[0].shape[1] // 2
    mine = me[0, 0] & (NX - 1)

    def step(y, carry):
        for d in range(peers):
            for k in range(2):
                start = pl.multiple_of(tables[d][0, 2 * (NX * y + mine) + k] * blk, blk)
                outs[d][y, k * blk : (k + 1) * blk, :] = column[y, pl.ds(start, blk), :]
        return carry

    lax.fori_loop(0, column.shape[0], step, 0)


def shipper(held, out, sems):
    n = out.shape[0]
    size = n // PARTS

    def copy(p):
        part = pl.ds(p * size, size)
        return pltpu.make_async_copy(held.at[part], out.at[part], sems.at[p])

    def ship(c):
        if c and c % size == 0:
            copy(c // size - 1).start()
        if c == n - 1:
            copy(PARTS - 1).start()
            for p in range(PARTS):
                copy(p).wait()

    return ship


def plan_kernel(col_slots, me, slots, live, plan):
    mine = me[0, 0] & (NX - 1)
    shift = col_slots.bit_length() - 1
    spare = plan.shape[1] - 1

    def scan(b, counts):
        slot = slots[0, b]
        col = slot & (col_slots - 1)
        piece = (mine - (col >> 1)) & (NX - 1)
        late = (piece == NX // 2).astype(jnp.int32)
        count = jnp.where(late == 1, counts[1], counts[0])
        place = ((piece - (piece >> 1)) * (1 - late)) * (col_slots // NX)
        feat = place + ((col >> 3) << 1) + (col & 1)
        plan[3 * late, count] = b
        plan[3 * late + 1, count] = feat
        plan[3 * late + 2, count] = slot >> shift
        return counts[0] + 1 - late, counts[1] + late

    zero = jnp.int32(0)
    counts = lax.fori_loop(0, live[0, 0], scan, (zero, zero))
    for part in range(2):
        for u in range(GROUP):
            plan[3 * part, counts[part] + u] = 0
            plan[3 * part + 1, counts[part] + u] = 0
            plan[3 * part + 2, counts[part] + u] = ROWS
        plan[3 * part, spare] = (counts[part] + GROUP - 1) >> 3


def accumulate(plan, first, groups, ready, values, feats, acc):
    def group(g, carry):
        ready(g)
        for start in range(0, GROUP, BATCH):
            terms = []
            for u in range(start, start + BATCH):
                b = g * GROUP + u
                term = jnp.dot(
                    values[b], feats[plan[first + 1, b]], preferred_element_type=F32
                )
                terms.append((plan[first + 2, b], term))
            for row, term in terms:
                acc[row] += term
        return carry

    lax.fori_loop(0, groups, group, 0)


def early_kernel(
    me, plan, need, source, column, near, far, acc, late, values, arrived, sems, late_sems
):
    blk = values.shape[1]
    mine = me[0, 0] & (NX - 1)
    spare = plan.shape[1] - 1
    groups, late_groups = plan[0, spare], plan[3, spare]

    def starter(first, target, sem):
        def start(g, carry):
            for u in range(GROUP):
                b = g * GROUP + u
                pltpu.make_async_copy(source.at[plan[first, b]], target.at[b], sem.at[g]).start()
            return carry

        return start

    def waiter(target, sem):
        def wait(g):
            part = pl.ds(pl.multiple_of(g * GROUP, GROUP), GROUP)
            pltpu.make_async_copy(source.at[pl.ds(0, GROUP)], target.at[part], sem.at[g]).wait()

        return wait

    lax.fori_loop(0, groups, starter(0, values, sems), 0)
    lax.fori_loop(0, late_groups, starter(3, late, late_sems), 0)
    acc[...] = jnp.zeros_like(acc)
    count = near.shape[0]

    def place(y, carry):
        for k in range(2):
            start = pl.multiple_of(need[0, 2 * (NX * y + mine) + k] * blk, blk)
            arrived[2 * y + k] = column[y, pl.ds(start, blk), :]
            arrived[count + 2 * y + k] = near[2 * y + k]
            arrived[2 * count + 2 * y + k] = far[2 * y + k]
        return carry

    lax.fori_loop(0, column.shape[0], place, 0)
    accumulate(plan, 0, groups, waiter(values, sems), values, arrived, acc)
    done = waiter(late, late_sems)

    def finish(g, carry):
        done(g)
        return carry

    lax.fori_loop(0, late_groups, finish, 0)


def late_kernel(plan, row_need, early, values, arrived, out, acc, held, out_sems):
    n, _, width = out.shape
    blk = values.shape[1]
    spare = plan.shape[1] - 1
    acc[...] = jnp.zeros_like(acc)
    accumulate(plan, 3, plan[3, spare], lambda g: None, values, arrived, acc)
    sub = lax.broadcasted_iota(jnp.int32, (EXTRA, width), 0)
    ship = shipper(held, out, out_sems)
    for c in range(n):
        for k in range(2):
            total = early[2 * c + k] + acc[2 * c + k]
            held[c, k * blk : (k + 1) * blk, :] = total.astype(BF16)
        ids = jnp.where(sub < EXTRA // 2, row_need[c, 0], row_need[c, 1])
        held[c, 2 * blk :, :] = ids.astype(F32).astype(BF16)
        ship(c)


def load_groups(live, source, values, sems):
    groups = live[0, 0] >> 3

    def load(g):
        part = pl.ds(pl.multiple_of(g * GROUP, GROUP), GROUP)
        return pltpu.make_async_copy(source.at[part], values.at[part], sems.at[g])

    def start(g, carry):
        load(g).start()
        return carry

    lax.fori_loop(0, groups, start, 0)
    return groups, load


def middle_kernel(arrived, weight, upstream, act, out, local_term, back):
    n, rows, width = arrived.shape
    blk = (rows - EXTRA) // 2
    per_dev = upstream.shape[0] // blk
    ids = []
    for c in range(n):
        tail = arrived[c, 2 * blk :, :].astype(F32)
        ids.append((tail[0:1, :], tail[EXTRA // 2 : EXTRA // 2 + 1, :]))
    w = weight[...]
    total = jnp.zeros((width, width), F32)
    for q in range(per_dev):
        acc = jnp.zeros((blk, width), F32)
        for c in range(n):
            for k in range(2):
                term = arrived[c, k * blk : (k + 1) * blk, :].astype(F32)
                acc = acc + jnp.where(ids[c][k] == float(q), term, 0.0)
        a = acc.astype(BF16)
        pre = jnp.dot(a, w, preferred_element_type=F32)
        sig = jax.nn.sigmoid(pre)
        act[q * blk : (q + 1) * blk, :] = (pre * sig).astype(BF16)
        up = upstream[q * blk : (q + 1) * blk, :].astype(F32)
        grad = (up * sig * (1.0 + pre * (1.0 - sig))).astype(BF16)
        total = total + lax.dot_general(a, grad, (((0,), (0,)), ((), ())), preferred_element_type=F32)
        back[q] = lax.dot_general(
            grad, w, (((1,), (1,)), ((), ())), preferred_element_type=F32
        ).astype(BF16)
    local_term[...] = total
    for c in range(n):
        for k in range(2):
            chosen = back[0]
            for q in range(1, per_dev):
                chosen = jnp.where(ids[c][k].astype(BF16) == float(q), back[q], chosen)
            out[c, k * blk : (k + 1) * blk, :] = chosen


def backward_kernel(
    col_slots, slots, live, source, arrived, out, values, acc, held, load_sems, sems
):
    blk = values.shape[1]
    shift = col_slots.bit_length() - 1
    groups, load = load_groups(live, source, values, load_sems)
    acc[...] = jnp.zeros_like(acc)

    def group(g, carry):
        load(g).wait()
        for first in range(0, GROUP, BATCH):
            terms = []
            for u in range(first, first + BATCH):
                b = g * GROUP + u
                slot = slots[0, b]
                grads = arrived[slot >> shift]
                term = lax.dot_general(
                    values[b], grads, (((0,), (0,)), ((), ())), preferred_element_type=F32
                )
                terms.append((slot & (col_slots - 1), term))
            for col, term in terms:
                acc[col] += term
        return carry

    lax.fori_loop(0, groups, group, 0)
    ship = shipper(held, out, sems)
    for r in range(out.shape[0]):
        for k in range(2):
            held[r, k * blk : (k + 1) * blk, :] = acc[2 * r + k].astype(BF16)
        ship(r)


def final_kernel(me, asked, arrived, out, acc):
    n, rows, _ = arrived.shape
    blk = rows // 2
    mine = me[0, 0]
    acc[...] = jnp.zeros_like(acc)

    def step(r, carry):
        ring = (r - mine) & (NX - 1)
        place = ((r ^ mine) & ~(NX - 1)) | ring
        for k in range(2):
            term = arrived[r, k * blk : (k + 1) * blk, :].astype(F32)
            acc[asked[place, 2 * mine + k]] += term
        return carry

    lax.fori_loop(0, n, step, 0, unroll=2)
    for q in range(acc.shape[0]):
        out[q * blk : (q + 1) * blk, :] = acc[q].astype(BF16)


def on_device(features, out_grad, weight, block_values, block_slot, live_count, row_need, col_need):
    n_rows = lax.axis_size("gr")
    n_cols = lax.axis_size("gc")
    values = pltpu.with_memory_space_constraint(block_values[0, 0], pltpu.HBM)
    slot_total, blk, _ = values.shape
    local, width = features.shape[2:]
    cap = row_need.shape[3]
    per_dev = local // blk
    col_slots = n_rows * cap
    row_slots = n_cols * cap
    slots = block_slot[0]
    work = 2 * slot_total * blk * blk * width

    def swap(array, axis):
        return lax.all_to_all(array, axis, split_axis=0, concat_axis=0, tiled=True)

    def trade(array, axis, bit):
        pairs = [(i, i ^ bit) for i in range(lax.axis_size(axis))]
        return lax.ppermute(array, axis, pairs)

    def upper(axis, bit):
        return (lax.axis_index(axis) & bit) != 0

    n_y = n_rows // NX
    me = lax.axis_index("gr").astype(jnp.int32).reshape(1, 1)

    def along_x(array, shift):
        pairs = [(i, i - i % NX + (i + shift) % NX) for i in range(n_rows)]
        return lax.ppermute(array, "gr", pairs)

    copies = call(
        repeat_kernel,
        jax.ShapeDtypeStruct((n_y, local, width), BF16),
        [VMEM],
        [pltpu.SemaphoreType.DMA((n_y,))],
        moved=2 << 20,
        out_spec=HBM,
        grant=60,
    )(features[0, 0])
    column = lax.all_to_all(
        copies,
        "gr",
        split_axis=0,
        concat_axis=0,
        tiled=True,
        axis_index_groups=[[NX * y + x for y in range(n_y)] for x in range(NX)],
    )
    need = jnp.pad(col_need[0, 0].reshape(1, -1), ((0, 0), (0, 128 - col_slots)))
    tables = [along_x(need, -d) for d in range(1, NX)]
    chosen = call(
        pick_kernel,
        [jax.ShapeDtypeStruct((n_y, cap * blk, width), BF16) for _ in tables],
        [SMEM, *[SMEM for _ in tables], VMEM],
        moved=4 << 20,
        grant=PICK_GRANT,
    )(me, *tables, column)
    plan = call(
        functools.partial(plan_kernel, col_slots),
        jax.ShapeDtypeStruct((6, slot_total + 2 * GROUP), jnp.int32),
        [SMEM, SMEM, SMEM],
        out_spec=SMEM,
    )(me, slots, live_count)
    pieces = {}
    for d in (1, NX - 1, NX // 2):
        piece = along_x(chosen[d - 1], d)
        pieces[d] = piece.reshape(cap * n_y, blk, width)
    early, late = call(
        early_kernel,
        (
            jax.ShapeDtypeStruct((row_slots + 1, blk, width), F32),
            jax.ShapeDtypeStruct(values.shape, BF16),
        ),
        [SMEM, SMEM, SMEM, HBM, VMEM, VMEM, VMEM],
        [
            pltpu.VMEM(values.shape, BF16),
            pltpu.VMEM(((NX - 1) * cap * n_y, blk, width), BF16),
            pltpu.SemaphoreType.DMA((slot_total // GROUP,)),
            pltpu.SemaphoreType.DMA((slot_total // GROUP,)),
        ],
        flops=work,
        moved=8 << 20,
        grant=FORWARD_GRANT,
    )(me, plan, need, values, column, pieces[1], pieces[NX - 1])
    partial = call(
        late_kernel,
        pltpu.HBM((n_cols, cap * blk + EXTRA, width), BF16),
        [SMEM, SMEM, VMEM, VMEM, VMEM],
        [
            pltpu.VMEM((row_slots + 1, blk, width), F32),
            pltpu.VMEM((n_cols, cap * blk + EXTRA, width), BF16),
            pltpu.SemaphoreType.DMA((PARTS,)),
        ],
        flops=work // 4,
        moved=8 << 20,
        out_spec=HBM,
        grant=FORWARD_GRANT,
    )(plan, row_need[0, 0], early, late, pieces[NX // 2])
    asked = jnp.concatenate([need, *tables], axis=0)
    bit = 1
    while bit < n_y:
        other = trade(asked, "gr", bit * NX)
        asked = jnp.concatenate([asked, other], axis=0)
        bit *= 2
    partial = swap(partial, "gc")
    activated, back, term = call(
        middle_kernel,
        (
            jax.ShapeDtypeStruct((local, width), BF16),
            pltpu.HBM((n_cols, cap * blk, width), BF16),
            jax.ShapeDtypeStruct((width, width), F32),
        ),
        [VMEM, VMEM, VMEM],
        [pltpu.VMEM((per_dev, blk, width), BF16)],
        flops=work // 8,
        moved=4 << 20,
    )(partial, weight, out_grad[0, 0])
    back = swap(back, "gc")

    halved = []
    bit = 1
    while bit < n_rows:
        if len(halved) < 2:
            low, high = jnp.split(term, 2, axis=0)
            top = upper("gr", bit)
            term = jnp.where(top, high, low) + trade(jnp.where(top, low, high), "gr", bit)
            halved.append(bit)
        else:
            other = trade(term, "gr", bit)
            term = term + other
        bit *= 2
    bit = 1
    while bit < n_cols:
        term = term + trade(term, "gc", bit)
        bit *= 2
    for bit in reversed(halved):
        other = trade(term, "gr", bit)
        top = upper("gr", bit)
        term = jnp.concatenate([jnp.where(top, other, term), jnp.where(top, term, other)], axis=0)
    node_total = local * n_rows * n_cols
    weight_grad = term * float(node_total) ** (-0.5)

    returned = call(
        functools.partial(backward_kernel, col_slots),
        pltpu.HBM((n_rows, cap * blk, width), BF16),
        [SMEM, SMEM, HBM, VMEM],
        [
            pltpu.VMEM(values.shape, BF16),
            pltpu.VMEM((col_slots, blk, width), F32),
            pltpu.VMEM((n_rows, cap * blk, width), BF16),
            pltpu.SemaphoreType.DMA((slot_total // GROUP,)),
            pltpu.SemaphoreType.DMA((PARTS,)),
        ],
        flops=work,
        moved=8 << 20,
        out_spec=HBM,
        grant=BACKWARD_GRANT,
    )(slots, live_count, values, back.reshape(row_slots, blk, width))
    returned = swap(returned, "gr")
    input_grad = call(
        final_kernel,
        jax.ShapeDtypeStruct((local, width), BF16),
        [SMEM, SMEM, VMEM],
        [pltpu.VMEM((per_dev, blk, width), F32)],
        moved=4 << 20,
    )(me, asked, returned)
    return (
        activated.reshape(1, 1, local, width),
        weight_grad,
        input_grad.reshape(1, 1, local, width),
    )


def solution(mesh):
    placed = (
        P("gc", "gr", None, None),
        P("gr", "gc", None, None),
        P(),
        P("gr", "gc", None, None, None),
        P("gr", "gc", None),
        P("gr", "gc"),
        P("gr", "gc", None, None),
        P("gr", "gc", None, None),
    )

    return jax.shard_map(
        on_device,
        mesh=mesh,
        in_specs=placed,
        out_specs=(P("gr", "gc", None, None), P(), P("gc", "gr", None, None)),
        check_vma=False,
    )
```

```python
import functools

import jax
import jax.numpy as jnp
from jax import lax
from jax.experimental import pallas as pl
from jax.experimental.pallas import tpu as pltpu
from jax.sharding import PartitionSpec as P

F32 = jnp.float32
BF16 = jnp.bfloat16
EXTRA = 16
NX = 4
GROUP = 8
BATCH = 2
PARTS = 4
ROWS = 32
PICK_GRANT = 40
BACKWARD_GRANT = 40
FORWARD_GRANT = 40

VMEM = pl.BlockSpec(memory_space=pltpu.VMEM)
SMEM = pl.BlockSpec(memory_space=pltpu.SMEM)
HBM = pl.BlockSpec(memory_space=pltpu.HBM)


def call(kernel, out_shape, in_specs, scratch=(), flops=0, moved=0, out_spec=VMEM, grant=48):
    many = isinstance(out_shape, (tuple, list))
    return pl.pallas_call(
        kernel,
        out_shape=out_shape,
        in_specs=in_specs,
        out_specs=(out_spec,) * len(out_shape) if many else out_spec,
        scratch_shapes=list(scratch),
        cost_estimate=pl.CostEstimate(flops=flops, bytes_accessed=moved, transcendentals=0),
        compiler_params=pltpu.CompilerParams(vmem_limit_bytes=grant << 20),
    )


def repeat_kernel(feats, out, sems):
    n = out.shape[0]
    copies = [pltpu.make_async_copy(feats, out.at[y], sems.at[y]) for y in range(n)]
    for copy in copies:
        copy.start()
    for copy in copies:
        copy.wait()


def pick_kernel(me, *refs):
    peers = NX - 1
    tables, column, outs = refs[:peers], refs[peers], refs[peers + 1 :]
    blk = outs[0].shape[1] // 2
    mine = me[0, 0] & (NX - 1)

    def step(y, carry):
        for d in range(peers):
            for k in range(2):
                start = pl.multiple_of(tables[d][0, 2 * (NX * y + mine) + k] * blk, blk)
                outs[d][y, k * blk : (k + 1) * blk, :] = column[y, pl.ds(start, blk), :]
        return carry

    lax.fori_loop(0, column.shape[0], step, 0)


def shipper(held, out, sems):
    n = out.shape[0]
    size = n // PARTS

    def copy(p):
        part = pl.ds(p * size, size)
        return pltpu.make_async_copy(held.at[part], out.at[part], sems.at[p])

    def ship(c):
        if c and c % size == 0:
            copy(c // size - 1).start()
        if c == n - 1:
            copy(PARTS - 1).start()
            for p in range(PARTS):
                copy(p).wait()

    return ship


def plan_kernel(col_slots, me, slots, live, plan):
    mine = me[0, 0] & (NX - 1)
    shift = col_slots.bit_length() - 1
    spare = plan.shape[1] - 1

    def scan(b, counts):
        slot = slots[0, b]
        col = slot & (col_slots - 1)
        piece = (mine - (col >> 1)) & (NX - 1)
        late = piece & 1
        count = jnp.where(late == 1, counts[1], counts[0])
        feat = (piece >> 1) * (col_slots // NX) + ((col >> 3) << 1) + (col & 1)
        plan[3 * late, count] = b
        plan[3 * late + 1, count] = feat
        plan[3 * late + 2, count] = slot >> shift
        return counts[0] + 1 - late, counts[1] + late

    zero = jnp.int32(0)
    counts = lax.fori_loop(0, live[0, 0], scan, (zero, zero))
    for part in range(2):
        for u in range(GROUP):
            plan[3 * part, counts[part] + u] = 0
            plan[3 * part + 1, counts[part] + u] = 0
            plan[3 * part + 2, counts[part] + u] = ROWS
        plan[3 * part, spare] = (counts[part] + GROUP - 1) >> 3


def accumulate(plan, first, groups, ready, values, feats, acc):
    def group(g, carry):
        ready(g)
        for start in range(0, GROUP, BATCH):
            terms = []
            for u in range(start, start + BATCH):
                b = g * GROUP + u
                term = jnp.dot(
                    values[b], feats[plan[first + 1, b]], preferred_element_type=F32
                )
                terms.append((plan[first + 2, b], term))
            for row, term in terms:
                acc[row] += term
        return carry

    lax.fori_loop(0, groups, group, 0)


def early_kernel(
    me, plan, need, source, column, far, acc, late, values, arrived, sems, late_sems
):
    blk = values.shape[1]
    mine = me[0, 0] & (NX - 1)
    spare = plan.shape[1] - 1
    groups, late_groups = plan[0, spare], plan[3, spare]

    def starter(first, target, sem):
        def start(g, carry):
            for u in range(GROUP):
                b = g * GROUP + u
                pltpu.make_async_copy(source.at[plan[first, b]], target.at[b], sem.at[g]).start()
            return carry

        return start

    def waiter(target, sem):
        def wait(g):
            part = pl.ds(pl.multiple_of(g * GROUP, GROUP), GROUP)
            pltpu.make_async_copy(source.at[pl.ds(0, GROUP)], target.at[part], sem.at[g]).wait()

        return wait

    lax.fori_loop(0, groups, starter(0, values, sems), 0)
    lax.fori_loop(0, late_groups, starter(3, late, late_sems), 0)
    acc[...] = jnp.zeros_like(acc)
    count = far.shape[0]

    def place(y, carry):
        for k in range(2):
            start = pl.multiple_of(need[0, 2 * (NX * y + mine) + k] * blk, blk)
            arrived[2 * y + k] = column[y, pl.ds(start, blk), :]
            arrived[count + 2 * y + k] = far[2 * y + k]
        return carry

    lax.fori_loop(0, column.shape[0], place, 0)
    accumulate(plan, 0, groups, waiter(values, sems), values, arrived, acc)
    done = waiter(late, late_sems)

    def finish(g, carry):
        done(g)
        return carry

    lax.fori_loop(0, late_groups, finish, 0)


def late_kernel(plan, row_need, early, values, left, right, out, acc, arrived, held, out_sems):
    n, _, width = out.shape
    blk = values.shape[1]
    spare = plan.shape[1] - 1
    acc[...] = jnp.zeros_like(acc)
    count = left.shape[0]
    arrived[:count] = left[...]
    arrived[count:] = right[...]
    accumulate(plan, 3, plan[3, spare], lambda g: None, values, arrived, acc)
    sub = lax.broadcasted_iota(jnp.int32, (EXTRA, width), 0)
    ship = shipper(held, out, out_sems)
    for c in range(n):
        for k in range(2):
            total = early[2 * c + k] + acc[2 * c + k]
            held[c, k * blk : (k + 1) * blk, :] = total.astype(BF16)
        ids = jnp.where(sub < EXTRA // 2, row_need[c, 0], row_need[c, 1])
        held[c, 2 * blk :, :] = ids.astype(F32).astype(BF16)
        ship(c)


def load_groups(live, source, values, sems):
    groups = live[0, 0] >> 3

    def load(g):
        part = pl.ds(pl.multiple_of(g * GROUP, GROUP), GROUP)
        return pltpu.make_async_copy(source.at[part], values.at[part], sems.at[g])

    def start(g, carry):
        load(g).start()
        return carry

    lax.fori_loop(0, groups, start, 0)
    return groups, load


def middle_kernel(arrived, weight, upstream, act, out, local_term, back):
    n, rows, width = arrived.shape
    blk = (rows - EXTRA) // 2
    per_dev = upstream.shape[0] // blk
    ids = []
    for c in range(n):
        tail = arrived[c, 2 * blk :, :].astype(F32)
        ids.append((tail[0:1, :], tail[EXTRA // 2 : EXTRA // 2 + 1, :]))
    w = weight[...]
    total = jnp.zeros((width, width), F32)
    for q in range(per_dev):
        acc = jnp.zeros((blk, width), F32)
        for c in range(n):
            for k in range(2):
                term = arrived[c, k * blk : (k + 1) * blk, :].astype(F32)
                acc = acc + jnp.where(ids[c][k] == float(q), term, 0.0)
        a = acc.astype(BF16)
        pre = jnp.dot(a, w, preferred_element_type=F32)
        sig = jax.nn.sigmoid(pre)
        act[q * blk : (q + 1) * blk, :] = (pre * sig).astype(BF16)
        up = upstream[q * blk : (q + 1) * blk, :].astype(F32)
        grad = (up * sig * (1.0 + pre * (1.0 - sig))).astype(BF16)
        total = total + lax.dot_general(a, grad, (((0,), (0,)), ((), ())), preferred_element_type=F32)
        back[q] = lax.dot_general(
            grad, w, (((1,), (1,)), ((), ())), preferred_element_type=F32
        ).astype(BF16)
    local_term[...] = total
    for c in range(n):
        for k in range(2):
            chosen = back[0]
            for q in range(1, per_dev):
                chosen = jnp.where(ids[c][k].astype(BF16) == float(q), back[q], chosen)
            out[c, k * blk : (k + 1) * blk, :] = chosen


def backward_kernel(
    col_slots, slots, live, source, arrived, out, values, acc, held, load_sems, sems
):
    blk = values.shape[1]
    shift = col_slots.bit_length() - 1
    groups, load = load_groups(live, source, values, load_sems)
    acc[...] = jnp.zeros_like(acc)

    def group(g, carry):
        load(g).wait()
        for first in range(0, GROUP, BATCH):
            terms = []
            for u in range(first, first + BATCH):
                b = g * GROUP + u
                slot = slots[0, b]
                grads = arrived[slot >> shift]
                term = lax.dot_general(
                    values[b], grads, (((0,), (0,)), ((), ())), preferred_element_type=F32
                )
                terms.append((slot & (col_slots - 1), term))
            for col, term in terms:
                acc[col] += term
        return carry

    lax.fori_loop(0, groups, group, 0)
    ship = shipper(held, out, sems)
    for r in range(out.shape[0]):
        for k in range(2):
            held[r, k * blk : (k + 1) * blk, :] = acc[2 * r + k].astype(BF16)
        ship(r)


def final_kernel(me, asked, arrived, out, acc):
    n, rows, _ = arrived.shape
    blk = rows // 2
    mine = me[0, 0]
    acc[...] = jnp.zeros_like(acc)

    def step(r, carry):
        ring = (r - mine) & (NX - 1)
        place = ((r ^ mine) & ~(NX - 1)) | ring
        for k in range(2):
            term = arrived[r, k * blk : (k + 1) * blk, :].astype(F32)
            acc[asked[place, 2 * mine + k]] += term
        return carry

    lax.fori_loop(0, n, step, 0, unroll=2)
    for q in range(acc.shape[0]):
        out[q * blk : (q + 1) * blk, :] = acc[q].astype(BF16)


def on_device(features, out_grad, weight, block_values, block_slot, live_count, row_need, col_need):
    n_rows = lax.axis_size("gr")
    n_cols = lax.axis_size("gc")
    values = pltpu.with_memory_space_constraint(block_values[0, 0], pltpu.HBM)
    slot_total, blk, _ = values.shape
    local, width = features.shape[2:]
    cap = row_need.shape[3]
    per_dev = local // blk
    col_slots = n_rows * cap
    row_slots = n_cols * cap
    slots = block_slot[0]
    work = 2 * slot_total * blk * blk * width

    def swap(array, axis):
        return lax.all_to_all(array, axis, split_axis=0, concat_axis=0, tiled=True)

    def trade(array, axis, bit):
        pairs = [(i, i ^ bit) for i in range(lax.axis_size(axis))]
        return lax.ppermute(array, axis, pairs)

    def upper(axis, bit):
        return (lax.axis_index(axis) & bit) != 0

    n_y = n_rows // NX
    me = lax.axis_index("gr").astype(jnp.int32).reshape(1, 1)

    def along_x(array, shift):
        pairs = [(i, i - i % NX + (i + shift) % NX) for i in range(n_rows)]
        return lax.ppermute(array, "gr", pairs)

    copies = call(
        repeat_kernel,
        jax.ShapeDtypeStruct((n_y, local, width), BF16),
        [VMEM],
        [pltpu.SemaphoreType.DMA((n_y,))],
        moved=2 << 20,
        out_spec=HBM,
        grant=60,
    )(features[0, 0])
    column = lax.all_to_all(
        copies,
        "gr",
        split_axis=0,
        concat_axis=0,
        tiled=True,
        axis_index_groups=[[NX * y + x for y in range(n_y)] for x in range(NX)],
    )
    need = jnp.pad(col_need[0, 0].reshape(1, -1), ((0, 0), (0, 128 - col_slots)))
    tables = [along_x(need, -d) for d in range(1, NX)]
    chosen = call(
        pick_kernel,
        [jax.ShapeDtypeStruct((n_y, cap * blk, width), BF16) for _ in tables],
        [SMEM, *[SMEM for _ in tables], VMEM],
        moved=4 << 20,
        grant=PICK_GRANT,
    )(me, *tables, column)
    plan = call(
        functools.partial(plan_kernel, col_slots),
        jax.ShapeDtypeStruct((6, slot_total + 2 * GROUP), jnp.int32),
        [SMEM, SMEM, SMEM],
        out_spec=SMEM,
    )(me, slots, live_count)
    pieces = {}
    for d in (2, 1, 3):
        piece = along_x(chosen[d - 1], d)
        pieces[d] = piece.reshape(cap * n_y, blk, width)
    early, late = call(
        early_kernel,
        (
            jax.ShapeDtypeStruct((row_slots + 1, blk, width), F32),
            jax.ShapeDtypeStruct(values.shape, BF16),
        ),
        [SMEM, SMEM, SMEM, HBM, VMEM, VMEM],
        [
            pltpu.VMEM(values.shape, BF16),
            pltpu.VMEM((2 * cap * n_y, blk, width), BF16),
            pltpu.SemaphoreType.DMA((slot_total // GROUP,)),
            pltpu.SemaphoreType.DMA((slot_total // GROUP,)),
        ],
        flops=work,
        moved=8 << 20,
        grant=FORWARD_GRANT,
    )(me, plan, need, values, column, pieces[2])
    partial = call(
        late_kernel,
        pltpu.HBM((n_cols, cap * blk + EXTRA, width), BF16),
        [SMEM, SMEM, VMEM, VMEM, VMEM, VMEM],
        [
            pltpu.VMEM((row_slots + 1, blk, width), F32),
            pltpu.VMEM((2 * cap * n_y, blk, width), BF16),
            pltpu.VMEM((n_cols, cap * blk + EXTRA, width), BF16),
            pltpu.SemaphoreType.DMA((PARTS,)),
        ],
        flops=work // 2,
        moved=8 << 20,
        out_spec=HBM,
        grant=FORWARD_GRANT,
    )(plan, row_need[0, 0], early, late, pieces[1], pieces[3])
    asked = jnp.concatenate([need, *tables], axis=0)
    bit = 1
    while bit < n_y:
        other = trade(asked, "gr", bit * NX)
        asked = jnp.concatenate([asked, other], axis=0)
        bit *= 2
    partial = swap(partial, "gc")
    activated, back, term = call(
        middle_kernel,
        (
            jax.ShapeDtypeStruct((local, width), BF16),
            pltpu.HBM((n_cols, cap * blk, width), BF16),
            jax.ShapeDtypeStruct((width, width), F32),
        ),
        [VMEM, VMEM, VMEM],
        [pltpu.VMEM((per_dev, blk, width), BF16)],
        flops=work // 8,
        moved=4 << 20,
    )(partial, weight, out_grad[0, 0])
    back = swap(back, "gc")

    halved = [1, 2]
    for bit in halved:
        low, high = jnp.split(term, 2, axis=0)
        top = upper("gr", bit)
        term = jnp.where(top, high, low) + trade(jnp.where(top, low, high), "gr", bit)
    other = trade(term, "gr", 4)
    term = term + other
    others = [trade(term, "gr", bits) for bits in (8, 16, 24)]
    term = (term + others[0]) + (others[1] + others[2])
    bit = 1
    while bit < n_cols:
        term = term + trade(term, "gc", bit)
        bit *= 2
    for bit in reversed(halved):
        other = trade(term, "gr", bit)
        top = upper("gr", bit)
        term = jnp.concatenate([jnp.where(top, other, term), jnp.where(top, term, other)], axis=0)
    node_total = local * n_rows * n_cols
    weight_grad = term * float(node_total) ** (-0.5)

    returned = call(
        functools.partial(backward_kernel, col_slots),
        pltpu.HBM((n_rows, cap * blk, width), BF16),
        [SMEM, SMEM, HBM, VMEM],
        [
            pltpu.VMEM(values.shape, BF16),
            pltpu.VMEM((col_slots, blk, width), F32),
            pltpu.VMEM((n_rows, cap * blk, width), BF16),
            pltpu.SemaphoreType.DMA((slot_total // GROUP,)),
            pltpu.SemaphoreType.DMA((PARTS,)),
        ],
        flops=work,
        moved=8 << 20,
        out_spec=HBM,
        grant=BACKWARD_GRANT,
    )(slots, live_count, values, back.reshape(row_slots, blk, width))
    returned = swap(returned, "gr")
    input_grad = call(
        final_kernel,
        jax.ShapeDtypeStruct((local, width), BF16),
        [SMEM, SMEM, VMEM],
        [pltpu.VMEM((per_dev, blk, width), F32)],
        moved=4 << 20,
    )(me, asked, returned)
    return (
        activated.reshape(1, 1, local, width),
        weight_grad,
        input_grad.reshape(1, 1, local, width),
    )


def solution(mesh):
    placed = (
        P("gc", "gr", None, None),
        P("gr", "gc", None, None),
        P(),
        P("gr", "gc", None, None, None),
        P("gr", "gc", None),
        P("gr", "gc"),
        P("gr", "gc", None, None),
        P("gr", "gc", None, None),
    )

    return jax.shard_map(
        on_device,
        mesh=mesh,
        in_specs=placed,
        out_specs=(P("gr", "gc", None, None), P(), P("gc", "gr", None, None)),
        check_vma=False,
    )
```

```python
import functools

import jax
import jax.numpy as jnp
from jax import lax
from jax.experimental import pallas as pl
from jax.experimental.pallas import tpu as pltpu
from jax.sharding import PartitionSpec as P

F32 = jnp.float32
BF16 = jnp.bfloat16
EXTRA = 16
NX = 4
GROUP = 8
WIDE = 16
BATCH = 2
PARTS = 4
ROWS = 32
PICK_GRANT = 40
BACKWARD_GRANT = 40
FORWARD_GRANT = 40

VMEM = pl.BlockSpec(memory_space=pltpu.VMEM)
SMEM = pl.BlockSpec(memory_space=pltpu.SMEM)
HBM = pl.BlockSpec(memory_space=pltpu.HBM)


def call(kernel, out_shape, in_specs, scratch=(), flops=0, moved=0, out_spec=VMEM, grant=48):
    many = isinstance(out_shape, (tuple, list))
    return pl.pallas_call(
        kernel,
        out_shape=out_shape,
        in_specs=in_specs,
        out_specs=(out_spec,) * len(out_shape) if many else out_spec,
        scratch_shapes=list(scratch),
        cost_estimate=pl.CostEstimate(flops=flops, bytes_accessed=moved, transcendentals=0),
        compiler_params=pltpu.CompilerParams(vmem_limit_bytes=grant << 20),
    )


def repeat_kernel(feats, out, sems):
    n = out.shape[0]
    copies = [pltpu.make_async_copy(feats, out.at[y], sems.at[y]) for y in range(n)]
    for copy in copies:
        copy.start()
    for copy in copies:
        copy.wait()


def pick_kernel(me, *refs):
    peers = NX - 1
    tables, column, outs = refs[:peers], refs[peers], refs[peers + 1 :]
    blk = outs[0].shape[1] // 2
    mine = me[0, 0] & (NX - 1)

    def step(y, carry):
        for d in range(peers):
            for k in range(2):
                start = pl.multiple_of(tables[d][0, 2 * (NX * y + mine) + k] * blk, blk)
                outs[d][y, k * blk : (k + 1) * blk, :] = column[y, pl.ds(start, blk), :]
        return carry

    lax.fori_loop(0, column.shape[0], step, 0)


def shipper(held, out, sems):
    n = out.shape[0]
    size = n // PARTS

    def copy(p):
        part = pl.ds(p * size, size)
        return pltpu.make_async_copy(held.at[part], out.at[part], sems.at[p])

    def ship(c):
        if c and c % size == 0:
            copy(c // size - 1).start()
        if c == n - 1:
            copy(PARTS - 1).start()
            for p in range(PARTS):
                copy(p).wait()

    return ship


def plan_kernel(col_slots, me, slots, live, plan):
    mine = me[0, 0] & (NX - 1)
    shift = col_slots.bit_length() - 1
    spare = plan.shape[1] - 1

    def scan(b, counts):
        slot = slots[0, b]
        col = slot & (col_slots - 1)
        piece = (mine - (col >> 1)) & (NX - 1)
        late = piece & 1
        count = jnp.where(late == 1, counts[1], counts[0])
        feat = (piece >> 1) * (col_slots // NX) + ((col >> 3) << 1) + (col & 1)
        plan[3 * late, count] = b
        plan[3 * late + 1, count] = feat
        plan[3 * late + 2, count] = slot >> shift
        return counts[0] + 1 - late, counts[1] + late

    zero = jnp.int32(0)
    counts = lax.fori_loop(0, live[0, 0], scan, (zero, zero))
    for part in range(2):
        for u in range(GROUP):
            plan[3 * part, counts[part] + u] = 0
            plan[3 * part + 1, counts[part] + u] = 0
            plan[3 * part + 2, counts[part] + u] = ROWS
        plan[3 * part, spare] = (counts[part] + GROUP - 1) >> 3


def accumulate(plan, first, groups, ready, values, feats, acc):
    def group(g, carry):
        ready(g)
        for start in range(0, GROUP, BATCH):
            terms = []
            for u in range(start, start + BATCH):
                b = g * GROUP + u
                term = jnp.dot(
                    values[b], feats[plan[first + 1, b]], preferred_element_type=F32
                )
                terms.append((plan[first + 2, b], term))
            for row, term in terms:
                acc[row] += term
        return carry

    lax.fori_loop(0, groups, group, 0)


def early_kernel(
    me, plan, need, source, column, far, acc, late, values, arrived, sems, late_sems
):
    blk = values.shape[1]
    mine = me[0, 0] & (NX - 1)
    spare = plan.shape[1] - 1
    groups, late_groups = plan[0, spare], plan[3, spare]

    def starter(first, target, sem):
        def start(g, carry):
            for u in range(GROUP):
                b = g * GROUP + u
                pltpu.make_async_copy(source.at[plan[first, b]], target.at[b], sem.at[g]).start()
            return carry

        return start

    def waiter(target, sem):
        def wait(g):
            part = pl.ds(pl.multiple_of(g * GROUP, GROUP), GROUP)
            pltpu.make_async_copy(source.at[pl.ds(0, GROUP)], target.at[part], sem.at[g]).wait()

        return wait

    lax.fori_loop(0, groups, starter(0, values, sems), 0)
    lax.fori_loop(0, late_groups, starter(3, late, late_sems), 0)
    acc[...] = jnp.zeros_like(acc)
    count = far.shape[0]

    def place(y, carry):
        for k in range(2):
            start = pl.multiple_of(need[0, 2 * (NX * y + mine) + k] * blk, blk)
            arrived[2 * y + k] = column[y, pl.ds(start, blk), :]
            arrived[count + 2 * y + k] = far[2 * y + k]
        return carry

    lax.fori_loop(0, column.shape[0], place, 0)
    accumulate(plan, 0, groups, waiter(values, sems), values, arrived, acc)
    done = waiter(late, late_sems)

    def finish(g, carry):
        done(g)
        return carry

    lax.fori_loop(0, late_groups, finish, 0)


def late_kernel(plan, row_need, early, values, left, right, out, acc, arrived, held, out_sems):
    n, _, width = out.shape
    blk = values.shape[1]
    spare = plan.shape[1] - 1
    acc[...] = jnp.zeros_like(acc)
    count = left.shape[0]
    arrived[:count] = left[...]
    arrived[count:] = right[...]
    accumulate(plan, 3, plan[3, spare], lambda g: None, values, arrived, acc)
    sub = lax.broadcasted_iota(jnp.int32, (EXTRA, width), 0)
    ship = shipper(held, out, out_sems)
    for c in range(n):
        for k in range(2):
            total = early[2 * c + k] + acc[2 * c + k]
            held[c, k * blk : (k + 1) * blk, :] = total.astype(BF16)
        ids = jnp.where(sub < EXTRA // 2, row_need[c, 0], row_need[c, 1])
        held[c, 2 * blk :, :] = ids.astype(F32).astype(BF16)
        ship(c)


def load_groups(live, source, values, sems):
    groups = live[0, 0] >> 3

    def load(g):
        part = pl.ds(pl.multiple_of(g * GROUP, GROUP), GROUP)
        return pltpu.make_async_copy(source.at[part], values.at[part], sems.at[g])

    def start(g, carry):
        load(g).start()
        return carry

    lax.fori_loop(0, groups, start, 0)
    return groups, load


def middle_kernel(arrived, weight, upstream, act, out, local_term, back):
    n, rows, width = arrived.shape
    blk = (rows - EXTRA) // 2
    per_dev = upstream.shape[0] // blk
    ids = []
    for c in range(n):
        tail = arrived[c, 2 * blk :, :].astype(F32)
        ids.append((tail[0:1, :], tail[EXTRA // 2 : EXTRA // 2 + 1, :]))
    w = weight[...]
    total = jnp.zeros((width, width), F32)
    for q in range(per_dev):
        acc = jnp.zeros((blk, width), F32)
        for c in range(n):
            for k in range(2):
                term = arrived[c, k * blk : (k + 1) * blk, :].astype(F32)
                acc = acc + jnp.where(ids[c][k] == float(q), term, 0.0)
        a = acc.astype(BF16)
        pre = jnp.dot(a, w, preferred_element_type=F32)
        sig = jax.nn.sigmoid(pre)
        act[q * blk : (q + 1) * blk, :] = (pre * sig).astype(BF16)
        up = upstream[q * blk : (q + 1) * blk, :].astype(F32)
        grad = (up * sig * (1.0 + pre * (1.0 - sig))).astype(BF16)
        total = total + lax.dot_general(a, grad, (((0,), (0,)), ((), ())), preferred_element_type=F32)
        back[q] = lax.dot_general(
            grad, w, (((1,), (1,)), ((), ())), preferred_element_type=F32
        ).astype(BF16)
    local_term[...] = total
    for c in range(n):
        for k in range(2):
            chosen = back[0]
            for q in range(1, per_dev):
                chosen = jnp.where(ids[c][k].astype(BF16) == float(q), back[q], chosen)
            out[c, k * blk : (k + 1) * blk, :] = chosen


def backward_kernel(
    col_slots, slots, live, source, arrived, out, values, acc, held, load_sems, sems
):
    blk = values.shape[1]
    shift = col_slots.bit_length() - 1
    groups, load = load_groups(live, source, values, load_sems)
    acc[...] = jnp.zeros_like(acc)

    def group(g, carry):
        for part in range(WIDE // GROUP):
            load(g * (WIDE // GROUP) + part).wait()
        for first in range(0, WIDE, BATCH):
            terms = []
            for u in range(first, first + BATCH):
                b = g * WIDE + u
                slot = slots[0, b]
                grads = arrived[slot >> shift]
                term = lax.dot_general(
                    values[b], grads, (((0,), (0,)), ((), ())), preferred_element_type=F32
                )
                terms.append((slot & (col_slots - 1), term))
            for col, term in terms:
                acc[col] += term
        return carry

    lax.fori_loop(0, groups // (WIDE // GROUP), group, 0)
    ship = shipper(held, out, sems)
    for r in range(out.shape[0]):
        for k in range(2):
            held[r, k * blk : (k + 1) * blk, :] = acc[2 * r + k].astype(BF16)
        ship(r)


def final_kernel(me, asked, arrived, out, acc):
    n, rows, _ = arrived.shape
    blk = rows // 2
    mine = me[0, 0]
    acc[...] = jnp.zeros_like(acc)

    def step(r, carry):
        ring = (r - mine) & (NX - 1)
        place = ((r ^ mine) & ~(NX - 1)) | ring
        for k in range(2):
            term = arrived[r, k * blk : (k + 1) * blk, :].astype(F32)
            acc[asked[place, 2 * mine + k]] += term
        return carry

    lax.fori_loop(0, n, step, 0, unroll=2)
    for q in range(acc.shape[0]):
        out[q * blk : (q + 1) * blk, :] = acc[q].astype(BF16)


def on_device(features, out_grad, weight, block_values, block_slot, live_count, row_need, col_need):
    n_rows = lax.axis_size("gr")
    n_cols = lax.axis_size("gc")
    values = pltpu.with_memory_space_constraint(block_values[0, 0], pltpu.HBM)
    slot_total, blk, _ = values.shape
    local, width = features.shape[2:]
    cap = row_need.shape[3]
    per_dev = local // blk
    col_slots = n_rows * cap
    row_slots = n_cols * cap
    slots = block_slot[0]
    work = 2 * slot_total * blk * blk * width

    def swap(array, axis):
        return lax.all_to_all(array, axis, split_axis=0, concat_axis=0, tiled=True)

    def trade(array, axis, bit):
        pairs = [(i, i ^ bit) for i in range(lax.axis_size(axis))]
        return lax.ppermute(array, axis, pairs)

    def upper(axis, bit):
        return (lax.axis_index(axis) & bit) != 0

    n_y = n_rows // NX
    me = lax.axis_index("gr").astype(jnp.int32).reshape(1, 1)

    def along_x(array, shift):
        pairs = [(i, i - i % NX + (i + shift) % NX) for i in range(n_rows)]
        return lax.ppermute(array, "gr", pairs)

    copies = call(
        repeat_kernel,
        jax.ShapeDtypeStruct((n_y, local, width), BF16),
        [VMEM],
        [pltpu.SemaphoreType.DMA((n_y,))],
        moved=2 << 20,
        out_spec=HBM,
        grant=60,
    )(features[0, 0])
    column = lax.all_to_all(
        copies,
        "gr",
        split_axis=0,
        concat_axis=0,
        tiled=True,
        axis_index_groups=[[NX * y + x for y in range(n_y)] for x in range(NX)],
    )
    need = jnp.pad(col_need[0, 0].reshape(1, -1), ((0, 0), (0, 128 - col_slots)))
    tables = [along_x(need, -d) for d in range(1, NX)]
    chosen = call(
        pick_kernel,
        [jax.ShapeDtypeStruct((n_y, cap * blk, width), BF16) for _ in tables],
        [SMEM, *[SMEM for _ in tables], VMEM],
        moved=4 << 20,
        grant=PICK_GRANT,
    )(me, *tables, column)
    plan = call(
        functools.partial(plan_kernel, col_slots),
        jax.ShapeDtypeStruct((6, slot_total + 2 * GROUP), jnp.int32),
        [SMEM, SMEM, SMEM],
        out_spec=SMEM,
    )(me, slots, live_count)
    pieces = {}
    for d in (2, 1, 3):
        piece = along_x(chosen[d - 1], d)
        pieces[d] = piece.reshape(cap * n_y, blk, width)
    early, late = call(
        early_kernel,
        (
            jax.ShapeDtypeStruct((row_slots + 1, blk, width), F32),
            jax.ShapeDtypeStruct(values.shape, BF16),
        ),
        [SMEM, SMEM, SMEM, HBM, VMEM, VMEM],
        [
            pltpu.VMEM(values.shape, BF16),
            pltpu.VMEM((2 * cap * n_y, blk, width), BF16),
            pltpu.SemaphoreType.DMA((slot_total // GROUP,)),
            pltpu.SemaphoreType.DMA((slot_total // GROUP,)),
        ],
        flops=work,
        moved=8 << 20,
        grant=FORWARD_GRANT,
    )(me, plan, need, values, column, pieces[2])
    partial = call(
        late_kernel,
        pltpu.HBM((n_cols, cap * blk + EXTRA, width), BF16),
        [SMEM, SMEM, VMEM, VMEM, VMEM, VMEM],
        [
            pltpu.VMEM((row_slots + 1, blk, width), F32),
            pltpu.VMEM((2 * cap * n_y, blk, width), BF16),
            pltpu.VMEM((n_cols, cap * blk + EXTRA, width), BF16),
            pltpu.SemaphoreType.DMA((PARTS,)),
        ],
        flops=work // 2,
        moved=8 << 20,
        out_spec=HBM,
        grant=FORWARD_GRANT,
    )(plan, row_need[0, 0], early, late, pieces[1], pieces[3])
    asked = jnp.concatenate([need, *tables], axis=0)
    bit = 1
    while bit < n_y:
        other = trade(asked, "gr", bit * NX)
        asked = jnp.concatenate([asked, other], axis=0)
        bit *= 2
    partial = swap(partial, "gc")
    activated, back, term = call(
        middle_kernel,
        (
            jax.ShapeDtypeStruct((local, width), BF16),
            pltpu.HBM((n_cols, cap * blk, width), BF16),
            jax.ShapeDtypeStruct((width, width), F32),
        ),
        [VMEM, VMEM, VMEM],
        [pltpu.VMEM((per_dev, blk, width), BF16)],
        flops=work // 8,
        moved=4 << 20,
    )(partial, weight, out_grad[0, 0])
    back = swap(back, "gc")

    halved = [1, 2]
    for bit in halved:
        low, high = jnp.split(term, 2, axis=0)
        top = upper("gr", bit)
        term = jnp.where(top, high, low) + trade(jnp.where(top, low, high), "gr", bit)
    for bit in (4, 8, 16):
        other = trade(term, "gr", bit)
        term = term + other
    bit = 1
    while bit < n_cols:
        term = term + trade(term, "gc", bit)
        bit *= 2
    for bit in reversed(halved):
        other = trade(term, "gr", bit)
        top = upper("gr", bit)
        term = jnp.concatenate([jnp.where(top, other, term), jnp.where(top, term, other)], axis=0)
    node_total = local * n_rows * n_cols
    weight_grad = term * float(node_total) ** (-0.5)

    returned = call(
        functools.partial(backward_kernel, col_slots),
        pltpu.HBM((n_rows, cap * blk, width), BF16),
        [SMEM, SMEM, HBM, VMEM],
        [
            pltpu.VMEM(values.shape, BF16),
            pltpu.VMEM((col_slots, blk, width), F32),
            pltpu.VMEM((n_rows, cap * blk, width), BF16),
            pltpu.SemaphoreType.DMA((slot_total // GROUP,)),
            pltpu.SemaphoreType.DMA((PARTS,)),
        ],
        flops=work,
        moved=8 << 20,
        out_spec=HBM,
        grant=BACKWARD_GRANT,
    )(slots, live_count, values, back.reshape(row_slots, blk, width))
    returned = swap(returned, "gr")
    input_grad = call(
        final_kernel,
        jax.ShapeDtypeStruct((local, width), BF16),
        [SMEM, SMEM, VMEM],
        [pltpu.VMEM((per_dev, blk, width), F32)],
        moved=4 << 20,
    )(me, asked, returned)
    return (
        activated.reshape(1, 1, local, width),
        weight_grad,
        input_grad.reshape(1, 1, local, width),
    )


def solution(mesh):
    placed = (
        P("gc", "gr", None, None),
        P("gr", "gc", None, None),
        P(),
        P("gr", "gc", None, None, None),
        P("gr", "gc", None),
        P("gr", "gc"),
        P("gr", "gc", None, None),
        P("gr", "gc", None, None),
    )

    return jax.shard_map(
        on_device,
        mesh=mesh,
        in_specs=placed,
        out_specs=(P("gr", "gc", None, None), P(), P("gc", "gr", None, None)),
        check_vma=False,
    )
```

```python
import functools

import jax
import jax.numpy as jnp
from jax import lax
from jax.experimental import pallas as pl
from jax.experimental.pallas import tpu as pltpu
from jax.sharding import PartitionSpec as P

F32 = jnp.float32
BF16 = jnp.bfloat16
EXTRA = 16
NX = 4
GROUP = 8
WIDE = 16
BATCH = 2
PARTS = 4
ROWS = 32
PICK_GRANT = 40
BACKWARD_GRANT = 40
FORWARD_GRANT = 40

VMEM = pl.BlockSpec(memory_space=pltpu.VMEM)
SMEM = pl.BlockSpec(memory_space=pltpu.SMEM)
HBM = pl.BlockSpec(memory_space=pltpu.HBM)


def call(kernel, out_shape, in_specs, scratch=(), flops=0, moved=0, out_spec=VMEM, grant=48):
    many = isinstance(out_shape, (tuple, list))
    return pl.pallas_call(
        kernel,
        out_shape=out_shape,
        in_specs=in_specs,
        out_specs=(out_spec,) * len(out_shape) if many else out_spec,
        scratch_shapes=list(scratch),
        cost_estimate=pl.CostEstimate(flops=flops, bytes_accessed=moved, transcendentals=0),
        compiler_params=pltpu.CompilerParams(vmem_limit_bytes=grant << 20),
    )


def repeat_kernel(feats, out, sems):
    n = out.shape[0]
    copies = [pltpu.make_async_copy(feats, out.at[y], sems.at[y]) for y in range(n)]
    for copy in copies:
        copy.start()
    for copy in copies:
        copy.wait()


def own_kernel(me, *refs):
    peers = NX - 1
    tables, feats, outs = refs[:peers], refs[peers], refs[peers + 1 :]
    blk = outs[0].shape[0] // 2
    for d in range(peers):
        for k in range(2):
            start = pl.multiple_of(tables[d][0, 2 * me[0, 0] + k] * blk, blk)
            outs[d][k * blk : (k + 1) * blk, :] = feats[pl.ds(start, blk), :]


def pick_kernel(me, *refs):
    peers = NX - 1
    tables, column, outs = refs[:peers], refs[peers], refs[peers + 1 :]
    blk = outs[0].shape[1] // 2
    n = column.shape[0]
    mine, row = me[0, 0] & (NX - 1), me[0, 0] >> 2

    def step(i, carry):
        y = (row + i + 1) & (n - 1)
        for d in range(peers):
            for k in range(2):
                start = pl.multiple_of(tables[d][0, 2 * (NX * y + mine) + k] * blk, blk)
                outs[d][i, k * blk : (k + 1) * blk, :] = column[y, pl.ds(start, blk), :]
        return carry

    lax.fori_loop(0, n - 1, step, 0)


def shipper(held, out, sems):
    n = out.shape[0]
    size = n // PARTS

    def copy(p):
        part = pl.ds(p * size, size)
        return pltpu.make_async_copy(held.at[part], out.at[part], sems.at[p])

    def ship(c):
        if c and c % size == 0:
            copy(c // size - 1).start()
        if c == n - 1:
            copy(PARTS - 1).start()
            for p in range(PARTS):
                copy(p).wait()

    return ship


def plan_kernel(col_slots, me, slots, live, plan):
    mine, row = me[0, 0] & (NX - 1), me[0, 0] >> 2
    shift = col_slots.bit_length() - 1
    spare = plan.shape[1] - 1
    n_y = col_slots // (2 * NX)

    def scan(b, counts):
        slot = slots[0, b]
        col = slot & (col_slots - 1)
        piece = (mine - (col >> 1)) & (NX - 1)
        late = piece & 1
        count = jnp.where(late == 1, counts[1], counts[0])
        turn = ((col >> 3) - row) & (n_y - 1)
        feat = (piece >> 1) * (2 * n_y) + 2 * turn + (col & 1)
        plan[3 * late, count] = b
        plan[3 * late + 1, count] = feat
        plan[3 * late + 2, count] = slot >> shift
        return counts[0] + 1 - late, counts[1] + late

    zero = jnp.int32(0)
    counts = lax.fori_loop(0, live[0, 0], scan, (zero, zero))
    for part in range(2):
        for u in range(GROUP):
            plan[3 * part, counts[part] + u] = 0
            plan[3 * part + 1, counts[part] + u] = 0
            plan[3 * part + 2, counts[part] + u] = ROWS
        plan[3 * part, spare] = (counts[part] + GROUP - 1) >> 3


def accumulate(plan, first, groups, ready, values, feats, acc):
    def group(g, carry):
        ready(g)
        for start in range(0, GROUP, BATCH):
            terms = []
            for u in range(start, start + BATCH):
                b = g * GROUP + u
                term = jnp.dot(
                    values[b], feats[plan[first + 1, b]], preferred_element_type=F32
                )
                terms.append((plan[first + 2, b], term))
            for row, term in terms:
                acc[row] += term
        return carry

    lax.fori_loop(0, groups, group, 0)


def early_kernel(
    me, plan, need, source, column, far0, far, acc, late, values, arrived, sems, late_sems
):
    blk = values.shape[1]
    mine, row = me[0, 0] & (NX - 1), me[0, 0] >> 2
    spare = plan.shape[1] - 1
    groups, late_groups = plan[0, spare], plan[3, spare]

    def starter(first, target, sem):
        def start(g, carry):
            for u in range(GROUP):
                b = g * GROUP + u
                pltpu.make_async_copy(source.at[plan[first, b]], target.at[b], sem.at[g]).start()
            return carry

        return start

    def waiter(target, sem):
        def wait(g):
            part = pl.ds(pl.multiple_of(g * GROUP, GROUP), GROUP)
            pltpu.make_async_copy(source.at[pl.ds(0, GROUP)], target.at[part], sem.at[g]).wait()

        return wait

    lax.fori_loop(0, groups, starter(0, values, sems), 0)
    lax.fori_loop(0, late_groups, starter(3, late, late_sems), 0)
    acc[...] = jnp.zeros_like(acc)
    n_y = column.shape[0]

    def place(turn, carry):
        y = (row + turn) & (n_y - 1)
        for k in range(2):
            start = pl.multiple_of(need[0, 2 * (NX * y + mine) + k] * blk, blk)
            arrived[2 * turn + k] = column[y, pl.ds(start, blk), :]
        return carry

    lax.fori_loop(0, n_y, place, 0)
    arrived[2 * n_y : 2 * n_y + 2] = far0[...]
    arrived[2 * n_y + 2 :] = far[...]
    accumulate(plan, 0, groups, waiter(values, sems), values, arrived, acc)
    done = waiter(late, late_sems)

    def finish(g, carry):
        done(g)
        return carry

    lax.fori_loop(0, late_groups, finish, 0)


def late_kernel(
    plan, row_need, early, values, left0, left, right0, right, out, acc, arrived, held, out_sems
):
    n, _, width = out.shape
    blk = values.shape[1]
    spare = plan.shape[1] - 1
    acc[...] = jnp.zeros_like(acc)
    count = 2 + left.shape[0]
    arrived[:2] = left0[...]
    arrived[2:count] = left[...]
    arrived[count : count + 2] = right0[...]
    arrived[count + 2 :] = right[...]
    accumulate(plan, 3, plan[3, spare], lambda g: None, values, arrived, acc)
    sub = lax.broadcasted_iota(jnp.int32, (EXTRA, width), 0)
    ship = shipper(held, out, out_sems)
    for c in range(n):
        for k in range(2):
            total = early[2 * c + k] + acc[2 * c + k]
            held[c, k * blk : (k + 1) * blk, :] = total.astype(BF16)
        ids = jnp.where(sub < EXTRA // 2, row_need[c, 0], row_need[c, 1])
        held[c, 2 * blk :, :] = ids.astype(F32).astype(BF16)
        ship(c)


def load_groups(live, source, values, sems):
    groups = live[0, 0] >> 3

    def load(g):
        part = pl.ds(pl.multiple_of(g * GROUP, GROUP), GROUP)
        return pltpu.make_async_copy(source.at[part], values.at[part], sems.at[g])

    def start(g, carry):
        load(g).start()
        return carry

    lax.fori_loop(0, groups, start, 0)
    return groups, load


def middle_kernel(arrived, weight, upstream, act, out, local_term, back):
    n, rows, width = arrived.shape
    blk = (rows - EXTRA) // 2
    per_dev = upstream.shape[0] // blk
    ids = []
    for c in range(n):
        tail = arrived[c, 2 * blk :, :].astype(F32)
        ids.append((tail[0:1, :], tail[EXTRA // 2 : EXTRA // 2 + 1, :]))
    w = weight[...]
    total = jnp.zeros((width, width), F32)
    for q in range(per_dev):
        acc = jnp.zeros((blk, width), F32)
        for c in range(n):
            for k in range(2):
                term = arrived[c, k * blk : (k + 1) * blk, :].astype(F32)
                acc = acc + jnp.where(ids[c][k] == float(q), term, 0.0)
        a = acc.astype(BF16)
        pre = jnp.dot(a, w, preferred_element_type=F32)
        sig = jax.nn.sigmoid(pre)
        act[q * blk : (q + 1) * blk, :] = (pre * sig).astype(BF16)
        up = upstream[q * blk : (q + 1) * blk, :].astype(F32)
        grad = (up * sig * (1.0 + pre * (1.0 - sig))).astype(BF16)
        total = total + lax.dot_general(a, grad, (((0,), (0,)), ((), ())), preferred_element_type=F32)
        back[q] = lax.dot_general(
            grad, w, (((1,), (1,)), ((), ())), preferred_element_type=F32
        ).astype(BF16)
    local_term[...] = total
    for c in range(n):
        for k in range(2):
            chosen = back[0]
            for q in range(1, per_dev):
                chosen = jnp.where(ids[c][k].astype(BF16) == float(q), back[q], chosen)
            out[c, k * blk : (k + 1) * blk, :] = chosen


def backward_kernel(
    col_slots, slots, live, source, arrived, out, values, acc, held, load_sems, sems
):
    blk = values.shape[1]
    shift = col_slots.bit_length() - 1
    groups, load = load_groups(live, source, values, load_sems)
    acc[...] = jnp.zeros_like(acc)

    def group(g, carry):
        for part in range(WIDE // GROUP):
            load(g * (WIDE // GROUP) + part).wait()
        for first in range(0, WIDE, BATCH):
            terms = []
            for u in range(first, first + BATCH):
                b = g * WIDE + u
                slot = slots[0, b]
                grads = arrived[slot >> shift]
                term = lax.dot_general(
                    values[b], grads, (((0,), (0,)), ((), ())), preferred_element_type=F32
                )
                terms.append((slot & (col_slots - 1), term))
            for col, term in terms:
                acc[col] += term
        return carry

    lax.fori_loop(0, groups // (WIDE // GROUP), group, 0)
    ship = shipper(held, out, sems)
    for r in range(out.shape[0]):
        for k in range(2):
            held[r, k * blk : (k + 1) * blk, :] = acc[2 * r + k].astype(BF16)
        ship(r)


def final_kernel(me, asked, arrived, out, acc):
    n, rows, _ = arrived.shape
    blk = rows // 2
    mine = me[0, 0]
    acc[...] = jnp.zeros_like(acc)

    def step(r, carry):
        ring = (r - mine) & (NX - 1)
        place = ((r ^ mine) & ~(NX - 1)) | ring
        for k in range(2):
            term = arrived[r, k * blk : (k + 1) * blk, :].astype(F32)
            acc[asked[place, 2 * mine + k]] += term
        return carry

    lax.fori_loop(0, n, step, 0, unroll=2)
    for q in range(acc.shape[0]):
        out[q * blk : (q + 1) * blk, :] = acc[q].astype(BF16)


def on_device(features, out_grad, weight, block_values, block_slot, live_count, row_need, col_need):
    n_rows = lax.axis_size("gr")
    n_cols = lax.axis_size("gc")
    values = pltpu.with_memory_space_constraint(block_values[0, 0], pltpu.HBM)
    slot_total, blk, _ = values.shape
    local, width = features.shape[2:]
    cap = row_need.shape[3]
    per_dev = local // blk
    col_slots = n_rows * cap
    row_slots = n_cols * cap
    slots = block_slot[0]
    work = 2 * slot_total * blk * blk * width

    def swap(array, axis):
        return lax.all_to_all(array, axis, split_axis=0, concat_axis=0, tiled=True)

    def trade(array, axis, bit):
        pairs = [(i, i ^ bit) for i in range(lax.axis_size(axis))]
        return lax.ppermute(array, axis, pairs)

    def upper(axis, bit):
        return (lax.axis_index(axis) & bit) != 0

    n_y = n_rows // NX
    me = lax.axis_index("gr").astype(jnp.int32).reshape(1, 1)

    def along_x(array, shift):
        pairs = [(i, i - i % NX + (i + shift) % NX) for i in range(n_rows)]
        return lax.ppermute(array, "gr", pairs)

    copies = call(
        repeat_kernel,
        jax.ShapeDtypeStruct((n_y, local, width), BF16),
        [VMEM],
        [pltpu.SemaphoreType.DMA((n_y,))],
        moved=2 << 20,
        out_spec=HBM,
        grant=60,
    )(features[0, 0])
    column = lax.all_to_all(
        copies,
        "gr",
        split_axis=0,
        concat_axis=0,
        tiled=True,
        axis_index_groups=[[NX * y + x for y in range(n_y)] for x in range(NX)],
    )
    need = jnp.pad(col_need[0, 0].reshape(1, -1), ((0, 0), (0, 128 - col_slots)))
    tables = [along_x(need, -d) for d in range(1, NX)]
    own = call(
        own_kernel,
        [jax.ShapeDtypeStruct((cap * blk, width), BF16) for _ in tables],
        [SMEM, *[SMEM for _ in tables], VMEM],
        moved=1 << 20,
        grant=PICK_GRANT,
    )(me, *tables, features[0, 0])
    firsts = {}
    for d in (2, 1, 3):
        first = along_x(own[d - 1], d)
        firsts[d] = first.reshape(cap, blk, width)
    chosen = call(
        pick_kernel,
        [jax.ShapeDtypeStruct((n_y - 1, cap * blk, width), BF16) for _ in tables],
        [SMEM, *[SMEM for _ in tables], VMEM],
        moved=4 << 20,
        grant=PICK_GRANT,
    )(me, *tables, column)
    plan = call(
        functools.partial(plan_kernel, col_slots),
        jax.ShapeDtypeStruct((6, slot_total + 2 * GROUP), jnp.int32),
        [SMEM, SMEM, SMEM],
        out_spec=SMEM,
    )(me, slots, live_count)
    pieces = {}
    for d in (2, 1, 3):
        piece = along_x(chosen[d - 1], d)
        pieces[d] = piece.reshape(cap * (n_y - 1), blk, width)
    early, late = call(
        early_kernel,
        (
            jax.ShapeDtypeStruct((row_slots + 1, blk, width), F32),
            jax.ShapeDtypeStruct(values.shape, BF16),
        ),
        [SMEM, SMEM, SMEM, HBM, VMEM, VMEM, VMEM],
        [
            pltpu.VMEM(values.shape, BF16),
            pltpu.VMEM((2 * cap * n_y, blk, width), BF16),
            pltpu.SemaphoreType.DMA((slot_total // GROUP,)),
            pltpu.SemaphoreType.DMA((slot_total // GROUP,)),
        ],
        flops=work,
        moved=8 << 20,
        grant=FORWARD_GRANT,
    )(me, plan, need, values, column, firsts[2], pieces[2])
    partial = call(
        late_kernel,
        pltpu.HBM((n_cols, cap * blk + EXTRA, width), BF16),
        [SMEM, SMEM, VMEM, VMEM, VMEM, VMEM, VMEM, VMEM],
        [
            pltpu.VMEM((row_slots + 1, blk, width), F32),
            pltpu.VMEM((2 * cap * n_y, blk, width), BF16),
            pltpu.VMEM((n_cols, cap * blk + EXTRA, width), BF16),
            pltpu.SemaphoreType.DMA((PARTS,)),
        ],
        flops=work // 2,
        moved=8 << 20,
        out_spec=HBM,
        grant=FORWARD_GRANT,
    )(plan, row_need[0, 0], early, late, firsts[1], pieces[1], firsts[3], pieces[3])
    asked = jnp.concatenate([need, *tables], axis=0)
    bit = 1
    while bit < n_y:
        other = trade(asked, "gr", bit * NX)
        asked = jnp.concatenate([asked, other], axis=0)
        bit *= 2
    partial = swap(partial, "gc")
    activated, back, term = call(
        middle_kernel,
        (
            jax.ShapeDtypeStruct((local, width), BF16),
            pltpu.HBM((n_cols, cap * blk, width), BF16),
            jax.ShapeDtypeStruct((width, width), F32),
        ),
        [VMEM, VMEM, VMEM],
        [pltpu.VMEM((per_dev, blk, width), BF16)],
        flops=work // 8,
        moved=4 << 20,
    )(partial, weight, out_grad[0, 0])
    back = swap(back, "gc")

    halved = [1, 2]
    for bit in halved:
        low, high = jnp.split(term, 2, axis=0)
        top = upper("gr", bit)
        term = jnp.where(top, high, low) + trade(jnp.where(top, low, high), "gr", bit)
    for bit in (4, 8, 16):
        other = trade(term, "gr", bit)
        term = term + other
    bit = 1
    while bit < n_cols:
        term = term + trade(term, "gc", bit)
        bit *= 2
    for bit in reversed(halved):
        other = trade(term, "gr", bit)
        top = upper("gr", bit)
        term = jnp.concatenate([jnp.where(top, other, term), jnp.where(top, term, other)], axis=0)
    node_total = local * n_rows * n_cols
    weight_grad = term * float(node_total) ** (-0.5)

    returned = call(
        functools.partial(backward_kernel, col_slots),
        pltpu.HBM((n_rows, cap * blk, width), BF16),
        [SMEM, SMEM, HBM, VMEM],
        [
            pltpu.VMEM(values.shape, BF16),
            pltpu.VMEM((col_slots, blk, width), F32),
            pltpu.VMEM((n_rows, cap * blk, width), BF16),
            pltpu.SemaphoreType.DMA((slot_total // GROUP,)),
            pltpu.SemaphoreType.DMA((PARTS,)),
        ],
        flops=work,
        moved=8 << 20,
        out_spec=HBM,
        grant=BACKWARD_GRANT,
    )(slots, live_count, values, back.reshape(row_slots, blk, width))
    returned = swap(returned, "gr")
    input_grad = call(
        final_kernel,
        jax.ShapeDtypeStruct((local, width), BF16),
        [SMEM, SMEM, VMEM],
        [pltpu.VMEM((per_dev, blk, width), F32)],
        moved=4 << 20,
    )(me, asked, returned)
    return (
        activated.reshape(1, 1, local, width),
        weight_grad,
        input_grad.reshape(1, 1, local, width),
    )


def solution(mesh):
    placed = (
        P("gc", "gr", None, None),
        P("gr", "gc", None, None),
        P(),
        P("gr", "gc", None, None, None),
        P("gr", "gc", None),
        P("gr", "gc"),
        P("gr", "gc", None, None),
        P("gr", "gc", None, None),
    )

    return jax.shard_map(
        on_device,
        mesh=mesh,
        in_specs=placed,
        out_specs=(P("gr", "gc", None, None), P(), P("gc", "gr", None, None)),
        check_vma=False,
    )
```

```python
import functools

import jax
import jax.numpy as jnp
from jax import lax
from jax.experimental import pallas as pl
from jax.experimental.pallas import tpu as pltpu
from jax.sharding import PartitionSpec as P

F32 = jnp.float32
BF16 = jnp.bfloat16
EXTRA = 16
NX = 4
GROUP = 8
WIDE = 32
BATCH = 2
PARTS = 4
ROWS = 32
PICK_GRANT = 40
BACKWARD_GRANT = 40
FORWARD_GRANT = 40

VMEM = pl.BlockSpec(memory_space=pltpu.VMEM)
SMEM = pl.BlockSpec(memory_space=pltpu.SMEM)
HBM = pl.BlockSpec(memory_space=pltpu.HBM)


def call(kernel, out_shape, in_specs, scratch=(), flops=0, moved=0, out_spec=VMEM, grant=48):
    many = isinstance(out_shape, (tuple, list))
    return pl.pallas_call(
        kernel,
        out_shape=out_shape,
        in_specs=in_specs,
        out_specs=(out_spec,) * len(out_shape) if many else out_spec,
        scratch_shapes=list(scratch),
        cost_estimate=pl.CostEstimate(flops=flops, bytes_accessed=moved, transcendentals=0),
        compiler_params=pltpu.CompilerParams(vmem_limit_bytes=grant << 20),
    )


def repeat_kernel(feats, out, sems):
    n = out.shape[0]
    copies = [pltpu.make_async_copy(feats, out.at[y], sems.at[y]) for y in range(n)]
    for copy in copies:
        copy.start()
    for copy in copies:
        copy.wait()


def own_kernel(me, *refs):
    peers = NX - 1
    tables, feats, outs = refs[:peers], refs[peers], refs[peers + 1 :]
    blk = outs[0].shape[0] // 2
    for d in range(peers):
        for k in range(2):
            start = pl.multiple_of(tables[d][0, 2 * me[0, 0] + k] * blk, blk)
            outs[d][k * blk : (k + 1) * blk, :] = feats[pl.ds(start, blk), :]


def pick_kernel(me, *refs):
    peers = NX - 1
    tables, column, outs = refs[:peers], refs[peers], refs[peers + 1 :]
    blk = outs[0].shape[1] // 2
    n = column.shape[0]
    mine, row = me[0, 0] & (NX - 1), me[0, 0] >> 2

    def step(i, carry):
        y = (row + i + 1) & (n - 1)
        for d in range(peers):
            for k in range(2):
                start = pl.multiple_of(tables[d][0, 2 * (NX * y + mine) + k] * blk, blk)
                outs[d][i, k * blk : (k + 1) * blk, :] = column[y, pl.ds(start, blk), :]
        return carry

    lax.fori_loop(0, n - 1, step, 0)


def shipper(held, out, sems):
    n = out.shape[0]
    size = n // PARTS

    def copy(p):
        part = pl.ds(p * size, size)
        return pltpu.make_async_copy(held.at[part], out.at[part], sems.at[p])

    def ship(c):
        if c and c % size == 0:
            copy(c // size - 1).start()
        if c == n - 1:
            copy(PARTS - 1).start()
            for p in range(PARTS):
                copy(p).wait()

    return ship


def plan_kernel(col_slots, me, slots, live, plan):
    mine, row = me[0, 0] & (NX - 1), me[0, 0] >> 2
    shift = col_slots.bit_length() - 1
    spare = plan.shape[1] - 1
    n_y = col_slots // (2 * NX)

    def scan(b, counts):
        slot = slots[0, b]
        col = slot & (col_slots - 1)
        piece = (mine - (col >> 1)) & (NX - 1)
        late = piece & 1
        count = jnp.where(late == 1, counts[1], counts[0])
        turn = ((col >> 3) - row) & (n_y - 1)
        feat = (piece >> 1) * (2 * n_y) + 2 * turn + (col & 1)
        plan[3 * late, count] = b
        plan[3 * late + 1, count] = feat
        plan[3 * late + 2, count] = slot >> shift
        return counts[0] + 1 - late, counts[1] + late

    zero = jnp.int32(0)
    counts = lax.fori_loop(0, live[0, 0], scan, (zero, zero))
    for part in range(2):
        for u in range(GROUP):
            plan[3 * part, counts[part] + u] = 0
            plan[3 * part + 1, counts[part] + u] = 0
            plan[3 * part + 2, counts[part] + u] = ROWS
        plan[3 * part, spare] = (counts[part] + GROUP - 1) >> 3


def accumulate(plan, first, groups, ready, values, feats, acc):
    def take(g, count):
        for part in range(count):
            ready(g + part)
        for u in range(count * GROUP):
            b = g * GROUP + u
            term = jnp.dot(values[b], feats[plan[first + 1, b]], preferred_element_type=F32)
            acc[plan[first + 2, b]] += term

    def pair(g, carry):
        take(2 * g, 2)
        return carry

    def single(g, carry):
        take(groups - 1, 1)
        return carry

    lax.fori_loop(0, groups >> 1, pair, 0)
    lax.fori_loop(0, groups & 1, single, 0)


def early_kernel(
    me, plan, need, source, column, far0, far, acc, late, values, arrived, sems, late_sems
):
    blk = values.shape[1]
    mine, row = me[0, 0] & (NX - 1), me[0, 0] >> 2
    spare = plan.shape[1] - 1
    groups, late_groups = plan[0, spare], plan[3, spare]

    def starter(first, target, sem):
        def start(g, carry):
            for u in range(GROUP):
                b = g * GROUP + u
                pltpu.make_async_copy(source.at[plan[first, b]], target.at[b], sem.at[g]).start()
            return carry

        return start

    def waiter(target, sem):
        def wait(g):
            part = pl.ds(pl.multiple_of(g * GROUP, GROUP), GROUP)
            pltpu.make_async_copy(source.at[pl.ds(0, GROUP)], target.at[part], sem.at[g]).wait()

        return wait

    lax.fori_loop(0, groups, starter(0, values, sems), 0)
    lax.fori_loop(0, late_groups, starter(3, late, late_sems), 0)
    acc[...] = jnp.zeros_like(acc)
    n_y = column.shape[0]

    def place(turn, carry):
        y = (row + turn) & (n_y - 1)
        for k in range(2):
            start = pl.multiple_of(need[0, 2 * (NX * y + mine) + k] * blk, blk)
            arrived[2 * turn + k] = column[y, pl.ds(start, blk), :]
        return carry

    lax.fori_loop(0, n_y, place, 0)
    arrived[2 * n_y : 2 * n_y + 2] = far0[...]
    arrived[2 * n_y + 2 :] = far[...]
    accumulate(plan, 0, groups, waiter(values, sems), values, arrived, acc)
    done = waiter(late, late_sems)

    def finish(g, carry):
        done(g)
        return carry

    lax.fori_loop(0, late_groups, finish, 0)


def late_kernel(
    plan, row_need, early, values, left0, left, right0, right, out, acc, arrived, held, out_sems
):
    n, _, width = out.shape
    blk = values.shape[1]
    spare = plan.shape[1] - 1
    acc[...] = jnp.zeros_like(acc)
    count = 2 + left.shape[0]
    arrived[:2] = left0[...]
    arrived[2:count] = left[...]
    arrived[count : count + 2] = right0[...]
    arrived[count + 2 :] = right[...]
    accumulate(plan, 3, plan[3, spare], lambda g: None, values, arrived, acc)
    sub = lax.broadcasted_iota(jnp.int32, (EXTRA, width), 0)
    ship = shipper(held, out, out_sems)
    for c in range(n):
        for k in range(2):
            total = early[2 * c + k] + acc[2 * c + k]
            held[c, k * blk : (k + 1) * blk, :] = total.astype(BF16)
        ids = jnp.where(sub < EXTRA // 2, row_need[c, 0], row_need[c, 1])
        held[c, 2 * blk :, :] = ids.astype(F32).astype(BF16)
        ship(c)


def load_groups(live, source, values, sems):
    groups = live[0, 0] >> 3

    def load(g):
        part = pl.ds(pl.multiple_of(g * GROUP, GROUP), GROUP)
        return pltpu.make_async_copy(source.at[part], values.at[part], sems.at[g])

    def start(g, carry):
        load(g).start()
        return carry

    lax.fori_loop(0, groups, start, 0)
    return groups, load


def middle_kernel(arrived, weight, upstream, act, out, local_term, back):
    n, rows, width = arrived.shape
    blk = (rows - EXTRA) // 2
    per_dev = upstream.shape[0] // blk
    ids = []
    for c in range(n):
        tail = arrived[c, 2 * blk :, :].astype(F32)
        ids.append((tail[0:1, :], tail[EXTRA // 2 : EXTRA // 2 + 1, :]))
    w = weight[...]
    total = jnp.zeros((width, width), F32)
    for q in range(per_dev):
        acc = jnp.zeros((blk, width), F32)
        for c in range(n):
            for k in range(2):
                term = arrived[c, k * blk : (k + 1) * blk, :].astype(F32)
                acc = acc + jnp.where(ids[c][k] == float(q), term, 0.0)
        a = acc.astype(BF16)
        pre = jnp.dot(a, w, preferred_element_type=F32)
        sig = jax.nn.sigmoid(pre)
        act[q * blk : (q + 1) * blk, :] = (pre * sig).astype(BF16)
        up = upstream[q * blk : (q + 1) * blk, :].astype(F32)
        grad = (up * sig * (1.0 + pre * (1.0 - sig))).astype(BF16)
        total = total + lax.dot_general(a, grad, (((0,), (0,)), ((), ())), preferred_element_type=F32)
        back[q] = lax.dot_general(
            grad, w, (((1,), (1,)), ((), ())), preferred_element_type=F32
        ).astype(BF16)
    local_term[...] = total
    for c in range(n):
        for k in range(2):
            chosen = back[0]
            for q in range(1, per_dev):
                chosen = jnp.where(ids[c][k].astype(BF16) == float(q), back[q], chosen)
            out[c, k * blk : (k + 1) * blk, :] = chosen


def backward_kernel(
    col_slots, slots, live, source, arrived, out, values, acc, held, load_sems, sems
):
    blk = values.shape[1]
    shift = col_slots.bit_length() - 1
    groups, load = load_groups(live, source, values, load_sems)
    acc[...] = jnp.zeros_like(acc)

    def group(g, carry):
        for part in range(WIDE // GROUP):
            load(g * (WIDE // GROUP) + part).wait()
        for first in range(0, WIDE, BATCH):
            terms = []
            for u in range(first, first + BATCH):
                b = g * WIDE + u
                slot = slots[0, b]
                grads = arrived[slot >> shift]
                term = lax.dot_general(
                    values[b], grads, (((0,), (0,)), ((), ())), preferred_element_type=F32
                )
                terms.append((slot & (col_slots - 1), term))
            for col, term in terms:
                acc[col] += term
        return carry

    lax.fori_loop(0, groups // (WIDE // GROUP), group, 0)
    ship = shipper(held, out, sems)
    for r in range(out.shape[0]):
        for k in range(2):
            held[r, k * blk : (k + 1) * blk, :] = acc[2 * r + k].astype(BF16)
        ship(r)


def final_kernel(me, asked, arrived, out, acc, more):
    n, rows, _ = arrived.shape
    blk = rows // 2
    mine = me[0, 0]
    acc[...] = jnp.zeros_like(acc)
    more[...] = jnp.zeros_like(more)

    def step(r, carry):
        ring = (r - mine) & (NX - 1)
        place = ((r ^ mine) & ~(NX - 1)) | ring
        first = arrived[r, :blk, :].astype(F32)
        second = arrived[r, blk:, :].astype(F32)
        acc[asked[place, 2 * mine]] += first
        more[asked[place, 2 * mine + 1]] += second
        return carry

    lax.fori_loop(0, n, step, 0, unroll=4)
    for q in range(acc.shape[0]):
        out[q * blk : (q + 1) * blk, :] = (acc[q] + more[q]).astype(BF16)


def on_device(features, out_grad, weight, block_values, block_slot, live_count, row_need, col_need):
    n_rows = lax.axis_size("gr")
    n_cols = lax.axis_size("gc")
    values = pltpu.with_memory_space_constraint(block_values[0, 0], pltpu.HBM)
    slot_total, blk, _ = values.shape
    local, width = features.shape[2:]
    cap = row_need.shape[3]
    per_dev = local // blk
    col_slots = n_rows * cap
    row_slots = n_cols * cap
    slots = block_slot[0]
    work = 2 * slot_total * blk * blk * width

    def swap(array, axis):
        return lax.all_to_all(array, axis, split_axis=0, concat_axis=0, tiled=True)

    def trade(array, axis, bit):
        pairs = [(i, i ^ bit) for i in range(lax.axis_size(axis))]
        return lax.ppermute(array, axis, pairs)

    def upper(axis, bit):
        return (lax.axis_index(axis) & bit) != 0

    n_y = n_rows // NX
    me = lax.axis_index("gr").astype(jnp.int32).reshape(1, 1)

    def along_x(array, shift):
        pairs = [(i, i - i % NX + (i + shift) % NX) for i in range(n_rows)]
        return lax.ppermute(array, "gr", pairs)

    copies = call(
        repeat_kernel,
        jax.ShapeDtypeStruct((n_y, local, width), BF16),
        [VMEM],
        [pltpu.SemaphoreType.DMA((n_y,))],
        moved=2 << 20,
        out_spec=HBM,
        grant=60,
    )(features[0, 0])
    column = lax.all_to_all(
        copies,
        "gr",
        split_axis=0,
        concat_axis=0,
        tiled=True,
        axis_index_groups=[[NX * y + x for y in range(n_y)] for x in range(NX)],
    )
    need = jnp.pad(col_need[0, 0].reshape(1, -1), ((0, 0), (0, 128 - col_slots)))
    tables = [along_x(need, -d) for d in range(1, NX)]
    own = call(
        own_kernel,
        [jax.ShapeDtypeStruct((cap * blk, width), BF16) for _ in tables],
        [SMEM, *[SMEM for _ in tables], VMEM],
        moved=1 << 20,
        grant=PICK_GRANT,
    )(me, *tables, features[0, 0])
    firsts = {}
    for d in (2, 1, 3):
        first = along_x(own[d - 1], d)
        firsts[d] = first.reshape(cap, blk, width)
    chosen = call(
        pick_kernel,
        [jax.ShapeDtypeStruct((n_y - 1, cap * blk, width), BF16) for _ in tables],
        [SMEM, *[SMEM for _ in tables], VMEM],
        moved=4 << 20,
        grant=PICK_GRANT,
    )(me, *tables, column)
    plan = call(
        functools.partial(plan_kernel, col_slots),
        jax.ShapeDtypeStruct((6, slot_total + 2 * GROUP), jnp.int32),
        [SMEM, SMEM, SMEM],
        out_spec=SMEM,
    )(me, slots, live_count)
    pieces = {}
    for d in (2, 1, 3):
        piece = along_x(chosen[d - 1], d)
        pieces[d] = piece.reshape(cap * (n_y - 1), blk, width)
    early, late = call(
        early_kernel,
        (
            jax.ShapeDtypeStruct((row_slots + 1, blk, width), F32),
            jax.ShapeDtypeStruct(values.shape, BF16),
        ),
        [SMEM, SMEM, SMEM, HBM, VMEM, VMEM, VMEM],
        [
            pltpu.VMEM(values.shape, BF16),
            pltpu.VMEM((2 * cap * n_y, blk, width), BF16),
            pltpu.SemaphoreType.DMA((slot_total // GROUP,)),
            pltpu.SemaphoreType.DMA((slot_total // GROUP,)),
        ],
        flops=work,
        moved=8 << 20,
        grant=FORWARD_GRANT,
    )(me, plan, need, values, column, firsts[2], pieces[2])
    partial = call(
        late_kernel,
        pltpu.HBM((n_cols, cap * blk + EXTRA, width), BF16),
        [SMEM, SMEM, VMEM, VMEM, VMEM, VMEM, VMEM, VMEM],
        [
            pltpu.VMEM((row_slots + 1, blk, width), F32),
            pltpu.VMEM((2 * cap * n_y, blk, width), BF16),
            pltpu.VMEM((n_cols, cap * blk + EXTRA, width), BF16),
            pltpu.SemaphoreType.DMA((PARTS,)),
        ],
        flops=work // 2,
        moved=8 << 20,
        out_spec=HBM,
        grant=FORWARD_GRANT,
    )(plan, row_need[0, 0], early, late, firsts[1], pieces[1], firsts[3], pieces[3])
    asked = jnp.concatenate([need, *tables], axis=0)
    bit = 1
    while bit < n_y:
        other = trade(asked, "gr", bit * NX)
        asked = jnp.concatenate([asked, other], axis=0)
        bit *= 2
    partial = swap(partial, "gc")
    activated, back, term = call(
        middle_kernel,
        (
            jax.ShapeDtypeStruct((local, width), BF16),
            pltpu.HBM((n_cols, cap * blk, width), BF16),
            jax.ShapeDtypeStruct((width, width), F32),
        ),
        [VMEM, VMEM, VMEM],
        [pltpu.VMEM((per_dev, blk, width), BF16)],
        flops=work // 8,
        moved=4 << 20,
    )(partial, weight, out_grad[0, 0])
    back = swap(back, "gc")

    halved = [1, 2]
    for bit in halved:
        low, high = jnp.split(term, 2, axis=0)
        top = upper("gr", bit)
        term = jnp.where(top, high, low) + trade(jnp.where(top, low, high), "gr", bit)
    for bit in (4, 8, 16):
        other = trade(term, "gr", bit)
        term = term + other
    bit = 1
    while bit < n_cols:
        term = term + trade(term, "gc", bit)
        bit *= 2
    for bit in reversed(halved):
        other = trade(term, "gr", bit)
        top = upper("gr", bit)
        term = jnp.concatenate([jnp.where(top, other, term), jnp.where(top, term, other)], axis=0)
    node_total = local * n_rows * n_cols
    weight_grad = term * float(node_total) ** (-0.5)

    returned = call(
        functools.partial(backward_kernel, col_slots),
        pltpu.HBM((n_rows, cap * blk, width), BF16),
        [SMEM, SMEM, HBM, VMEM],
        [
            pltpu.VMEM(values.shape, BF16),
            pltpu.VMEM((col_slots, blk, width), F32),
            pltpu.VMEM((n_rows, cap * blk, width), BF16),
            pltpu.SemaphoreType.DMA((slot_total // GROUP,)),
            pltpu.SemaphoreType.DMA((PARTS,)),
        ],
        flops=work,
        moved=8 << 20,
        out_spec=HBM,
        grant=BACKWARD_GRANT,
    )(slots, live_count, values, back.reshape(row_slots, blk, width))
    returned = swap(returned, "gr")
    input_grad = call(
        final_kernel,
        jax.ShapeDtypeStruct((local, width), BF16),
        [SMEM, SMEM, VMEM],
        [pltpu.VMEM((per_dev, blk, width), F32), pltpu.VMEM((per_dev, blk, width), F32)],
        moved=4 << 20,
    )(me, asked, returned)
    return (
        activated.reshape(1, 1, local, width),
        weight_grad,
        input_grad.reshape(1, 1, local, width),
    )


def solution(mesh):
    placed = (
        P("gc", "gr", None, None),
        P("gr", "gc", None, None),
        P(),
        P("gr", "gc", None, None, None),
        P("gr", "gc", None),
        P("gr", "gc"),
        P("gr", "gc", None, None),
        P("gr", "gc", None, None),
    )

    return jax.shard_map(
        on_device,
        mesh=mesh,
        in_specs=placed,
        out_specs=(P("gr", "gc", None, None), P(), P("gc", "gr", None, None)),
        check_vma=False,
    )
```

```python
import functools

import jax
import jax.numpy as jnp
from jax import lax
from jax.experimental import pallas as pl
from jax.experimental.pallas import tpu as pltpu
from jax.sharding import PartitionSpec as P

F32 = jnp.float32
BF16 = jnp.bfloat16
EXTRA = 16
NX = 4
GROUP = 8
WIDE = 32
BATCH = 2
PARTS = 4
ROWS = 32
PICK_GRANT = 40
BACKWARD_GRANT = 40
FORWARD_GRANT = 40

VMEM = pl.BlockSpec(memory_space=pltpu.VMEM)
SMEM = pl.BlockSpec(memory_space=pltpu.SMEM)
HBM = pl.BlockSpec(memory_space=pltpu.HBM)


def call(kernel, out_shape, in_specs, scratch=(), flops=0, moved=0, out_spec=VMEM, grant=48):
    many = isinstance(out_shape, (tuple, list))
    return pl.pallas_call(
        kernel,
        out_shape=out_shape,
        in_specs=in_specs,
        out_specs=(out_spec,) * len(out_shape) if many else out_spec,
        scratch_shapes=list(scratch),
        cost_estimate=pl.CostEstimate(flops=flops, bytes_accessed=moved, transcendentals=0),
        compiler_params=pltpu.CompilerParams(vmem_limit_bytes=grant << 20),
    )


def repeat_kernel(feats, out, held, load_sems, sems):
    n = out.shape[0]
    size = feats.shape[0] // PARTS
    parts = [pl.ds(p * size, size) for p in range(PARTS)]
    loads = [pltpu.make_async_copy(feats.at[p], held.at[p], load_sems.at[i]) for i, p in enumerate(parts)]
    for load in loads:
        load.start()
    copies = []
    for i, p in enumerate(parts):
        loads[i].wait()
        for y in range(n):
            copies.append(pltpu.make_async_copy(held.at[p], out.at[y, p], sems.at[i, y]))
            copies[-1].start()
    for copy in copies:
        copy.wait()


def own_kernel(me, *refs):
    peers = NX - 1
    tables, feats, outs = refs[:peers], refs[peers], refs[peers + 1 :]
    blk = outs[0].shape[0] // 2
    for d in range(peers):
        for k in range(2):
            start = pl.multiple_of(tables[d][0, 2 * me[0, 0] + k] * blk, blk)
            outs[d][k * blk : (k + 1) * blk, :] = feats[pl.ds(start, blk), :]


def pick_kernel(me, *refs):
    peers = NX - 1
    tables, column, outs = refs[:peers], refs[peers], refs[peers + 1 :]
    blk = outs[0].shape[1] // 2
    n = column.shape[0]
    mine, row = me[0, 0] & (NX - 1), me[0, 0] >> 2

    def step(i, carry):
        y = (row + i + 1) & (n - 1)
        for d in range(peers):
            for k in range(2):
                start = pl.multiple_of(tables[d][0, 2 * (NX * y + mine) + k] * blk, blk)
                outs[d][i, k * blk : (k + 1) * blk, :] = column[y, pl.ds(start, blk), :]
        return carry

    lax.fori_loop(0, n - 1, step, 0)


def shipper(held, out, sems):
    n = out.shape[0]
    size = n // PARTS

    def copy(p):
        part = pl.ds(p * size, size)
        return pltpu.make_async_copy(held.at[part], out.at[part], sems.at[p])

    def ship(c):
        if c and c % size == 0:
            copy(c // size - 1).start()
        if c == n - 1:
            copy(PARTS - 1).start()
            for p in range(PARTS):
                copy(p).wait()

    return ship


def plan_kernel(col_slots, me, slots, live, plan):
    mine, row = me[0, 0] & (NX - 1), me[0, 0] >> 2
    shift = col_slots.bit_length() - 1
    spare = plan.shape[1] - 1
    n_y = col_slots // (2 * NX)

    def scan(b, counts):
        slot = slots[0, b]
        col = slot & (col_slots - 1)
        piece = (mine - (col >> 1)) & (NX - 1)
        late = piece & 1
        count = jnp.where(late == 1, counts[1], counts[0])
        turn = ((col >> 3) - row) & (n_y - 1)
        feat = (piece >> 1) * (2 * n_y) + 2 * turn + (col & 1)
        plan[3 * late, count] = b
        plan[3 * late + 1, count] = feat
        plan[3 * late + 2, count] = slot >> shift
        return counts[0] + 1 - late, counts[1] + late

    zero = jnp.int32(0)
    counts = lax.fori_loop(0, live[0, 0], scan, (zero, zero))
    for part in range(2):
        for u in range(GROUP):
            plan[3 * part, counts[part] + u] = 0
            plan[3 * part + 1, counts[part] + u] = 0
            plan[3 * part + 2, counts[part] + u] = ROWS
        plan[3 * part, spare] = (counts[part] + GROUP - 1) >> 3


def accumulate(plan, first, groups, ready, values, feats, acc):
    def take(g, count):
        for part in range(count):
            ready(g + part)
        for u in range(count * GROUP):
            b = g * GROUP + u
            term = jnp.dot(values[b], feats[plan[first + 1, b]], preferred_element_type=F32)
            acc[plan[first + 2, b]] += term

    def pair(g, carry):
        take(2 * g, 2)
        return carry

    def single(g, carry):
        take(groups - 1, 1)
        return carry

    lax.fori_loop(0, groups >> 1, pair, 0)
    lax.fori_loop(0, groups & 1, single, 0)


def early_kernel(
    me, plan, need, source, column, far0, far, acc, late, values, arrived, sems, late_sems
):
    blk = values.shape[1]
    mine, row = me[0, 0] & (NX - 1), me[0, 0] >> 2
    spare = plan.shape[1] - 1
    groups, late_groups = plan[0, spare], plan[3, spare]

    def starter(first, target, sem):
        def start(g, carry):
            for u in range(GROUP):
                b = g * GROUP + u
                pltpu.make_async_copy(source.at[plan[first, b]], target.at[b], sem.at[g]).start()
            return carry

        return start

    def waiter(target, sem):
        def wait(g):
            part = pl.ds(pl.multiple_of(g * GROUP, GROUP), GROUP)
            pltpu.make_async_copy(source.at[pl.ds(0, GROUP)], target.at[part], sem.at[g]).wait()

        return wait

    lax.fori_loop(0, groups, starter(0, values, sems), 0)
    lax.fori_loop(0, late_groups, starter(3, late, late_sems), 0)
    acc[...] = jnp.zeros_like(acc)
    n_y = column.shape[0]

    def place(turn, carry):
        y = (row + turn) & (n_y - 1)
        for k in range(2):
            start = pl.multiple_of(need[0, 2 * (NX * y + mine) + k] * blk, blk)
            arrived[2 * turn + k] = column[y, pl.ds(start, blk), :]
        return carry

    lax.fori_loop(0, n_y, place, 0)
    arrived[2 * n_y : 2 * n_y + 2] = far0[...]
    arrived[2 * n_y + 2 :] = far[...]
    accumulate(plan, 0, groups, waiter(values, sems), values, arrived, acc)
    done = waiter(late, late_sems)

    def finish(g, carry):
        done(g)
        return carry

    lax.fori_loop(0, late_groups, finish, 0)


def late_kernel(
    plan, row_need, early, values, left0, left, right0, right, out, acc, arrived, held, out_sems
):
    n, _, width = out.shape
    blk = values.shape[1]
    spare = plan.shape[1] - 1
    acc[...] = jnp.zeros_like(acc)
    count = 2 + left.shape[0]
    arrived[:2] = left0[...]
    arrived[2:count] = left[...]
    arrived[count : count + 2] = right0[...]
    arrived[count + 2 :] = right[...]
    accumulate(plan, 3, plan[3, spare], lambda g: None, values, arrived, acc)
    sub = lax.broadcasted_iota(jnp.int32, (EXTRA, width), 0)
    ship = shipper(held, out, out_sems)
    for c in range(n):
        for k in range(2):
            total = early[2 * c + k] + acc[2 * c + k]
            held[c, k * blk : (k + 1) * blk, :] = total.astype(BF16)
        ids = jnp.where(sub < EXTRA // 2, row_need[c, 0], row_need[c, 1])
        held[c, 2 * blk :, :] = ids.astype(F32).astype(BF16)
        ship(c)


def load_groups(live, source, values, sems):
    groups = live[0, 0] >> 3

    def load(g):
        part = pl.ds(pl.multiple_of(g * GROUP, GROUP), GROUP)
        return pltpu.make_async_copy(source.at[part], values.at[part], sems.at[g])

    def start(g, carry):
        load(g).start()
        return carry

    lax.fori_loop(0, groups, start, 0)
    return groups, load


def middle_kernel(arrived, weight, upstream, act, out, local_term, back):
    n, rows, width = arrived.shape
    blk = (rows - EXTRA) // 2
    per_dev = upstream.shape[0] // blk
    ids = []
    for c in range(n):
        tail = arrived[c, 2 * blk :, :].astype(F32)
        ids.append((tail[0:1, :], tail[EXTRA // 2 : EXTRA // 2 + 1, :]))
    w = weight[...]
    total = jnp.zeros((width, width), F32)
    for q in range(per_dev):
        acc = jnp.zeros((blk, width), F32)
        for c in range(n):
            for k in range(2):
                term = arrived[c, k * blk : (k + 1) * blk, :].astype(F32)
                acc = acc + jnp.where(ids[c][k] == float(q), term, 0.0)
        a = acc.astype(BF16)
        pre = jnp.dot(a, w, preferred_element_type=F32)
        sig = jax.nn.sigmoid(pre)
        act[q * blk : (q + 1) * blk, :] = (pre * sig).astype(BF16)
        up = upstream[q * blk : (q + 1) * blk, :].astype(F32)
        grad = (up * sig * (1.0 + pre * (1.0 - sig))).astype(BF16)
        total = total + lax.dot_general(a, grad, (((0,), (0,)), ((), ())), preferred_element_type=F32)
        back[q] = lax.dot_general(
            grad, w, (((1,), (1,)), ((), ())), preferred_element_type=F32
        ).astype(BF16)
    local_term[...] = total
    for c in range(n):
        for k in range(2):
            chosen = back[0]
            for q in range(1, per_dev):
                chosen = jnp.where(ids[c][k].astype(BF16) == float(q), back[q], chosen)
            out[c, k * blk : (k + 1) * blk, :] = chosen


def backward_kernel(
    col_slots, slots, live, source, arrived, out, values, acc, held, load_sems, sems
):
    blk = values.shape[1]
    shift = col_slots.bit_length() - 1
    groups, load = load_groups(live, source, values, load_sems)
    acc[...] = jnp.zeros_like(acc)

    def group(g, carry):
        for part in range(WIDE // GROUP):
            load(g * (WIDE // GROUP) + part).wait()
        for first in range(0, WIDE, BATCH):
            terms = []
            for u in range(first, first + BATCH):
                b = g * WIDE + u
                slot = slots[0, b]
                grads = arrived[slot >> shift]
                term = lax.dot_general(
                    values[b], grads, (((0,), (0,)), ((), ())), preferred_element_type=F32
                )
                terms.append((slot & (col_slots - 1), term))
            for col, term in terms:
                acc[col] += term
        return carry

    lax.fori_loop(0, groups // (WIDE // GROUP), group, 0)
    ship = shipper(held, out, sems)
    for r in range(out.shape[0]):
        for k in range(2):
            held[r, k * blk : (k + 1) * blk, :] = acc[2 * r + k].astype(BF16)
        ship(r)


def final_kernel(me, asked, arrived, out, acc, more):
    n, rows, _ = arrived.shape
    blk = rows // 2
    mine = me[0, 0]
    acc[...] = jnp.zeros_like(acc)
    more[...] = jnp.zeros_like(more)

    def step(r, carry):
        ring = (r - mine) & (NX - 1)
        place = ((r ^ mine) & ~(NX - 1)) | ring
        first = arrived[r, :blk, :].astype(F32)
        second = arrived[r, blk:, :].astype(F32)
        acc[asked[place, 2 * mine]] += first
        more[asked[place, 2 * mine + 1]] += second
        return carry

    lax.fori_loop(0, n, step, 0, unroll=4)
    for q in range(acc.shape[0]):
        out[q * blk : (q + 1) * blk, :] = (acc[q] + more[q]).astype(BF16)


def on_device(features, out_grad, weight, block_values, block_slot, live_count, row_need, col_need):
    n_rows = lax.axis_size("gr")
    n_cols = lax.axis_size("gc")
    values = pltpu.with_memory_space_constraint(block_values[0, 0], pltpu.HBM)
    slot_total, blk, _ = values.shape
    local, width = features.shape[2:]
    cap = row_need.shape[3]
    per_dev = local // blk
    col_slots = n_rows * cap
    row_slots = n_cols * cap
    slots = block_slot[0]
    work = 2 * slot_total * blk * blk * width

    def swap(array, axis):
        return lax.all_to_all(array, axis, split_axis=0, concat_axis=0, tiled=True)

    def trade(array, axis, bit):
        pairs = [(i, i ^ bit) for i in range(lax.axis_size(axis))]
        return lax.ppermute(array, axis, pairs)

    def upper(axis, bit):
        return (lax.axis_index(axis) & bit) != 0

    n_y = n_rows // NX
    me = lax.axis_index("gr").astype(jnp.int32).reshape(1, 1)

    def along_x(array, shift):
        pairs = [(i, i - i % NX + (i + shift) % NX) for i in range(n_rows)]
        return lax.ppermute(array, "gr", pairs)

    copies = call(
        repeat_kernel,
        jax.ShapeDtypeStruct((n_y, local, width), BF16),
        [HBM],
        [
            pltpu.VMEM((local, width), BF16),
            pltpu.SemaphoreType.DMA((PARTS,)),
            pltpu.SemaphoreType.DMA((PARTS, n_y)),
        ],
        moved=2 << 20,
        out_spec=HBM,
        grant=60,
    )(features[0, 0])
    column = lax.all_to_all(
        copies,
        "gr",
        split_axis=0,
        concat_axis=0,
        tiled=True,
        axis_index_groups=[[NX * y + x for y in range(n_y)] for x in range(NX)],
    )
    need = jnp.pad(col_need[0, 0].reshape(1, -1), ((0, 0), (0, 128 - col_slots)))
    tables = [along_x(need, -d) for d in range(1, NX)]
    own = call(
        own_kernel,
        [jax.ShapeDtypeStruct((cap * blk, width), BF16) for _ in tables],
        [SMEM, *[SMEM for _ in tables], VMEM],
        moved=1 << 20,
        grant=PICK_GRANT,
    )(me, *tables, features[0, 0])
    firsts = {}
    for d in (2, 1, 3):
        first = along_x(own[d - 1], d)
        firsts[d] = first.reshape(cap, blk, width)
    chosen = call(
        pick_kernel,
        [jax.ShapeDtypeStruct((n_y - 1, cap * blk, width), BF16) for _ in tables],
        [SMEM, *[SMEM for _ in tables], VMEM],
        moved=4 << 20,
        grant=PICK_GRANT,
    )(me, *tables, column)
    plan = call(
        functools.partial(plan_kernel, col_slots),
        jax.ShapeDtypeStruct((6, slot_total + 2 * GROUP), jnp.int32),
        [SMEM, SMEM, SMEM],
        out_spec=SMEM,
    )(me, slots, live_count)
    pieces = {}
    for d in (2, 1, 3):
        piece = along_x(chosen[d - 1], d)
        pieces[d] = piece.reshape(cap * (n_y - 1), blk, width)
    early, late = call(
        early_kernel,
        (
            jax.ShapeDtypeStruct((row_slots + 1, blk, width), F32),
            jax.ShapeDtypeStruct(values.shape, BF16),
        ),
        [SMEM, SMEM, SMEM, HBM, VMEM, VMEM, VMEM],
        [
            pltpu.VMEM(values.shape, BF16),
            pltpu.VMEM((2 * cap * n_y, blk, width), BF16),
            pltpu.SemaphoreType.DMA((slot_total // GROUP,)),
            pltpu.SemaphoreType.DMA((slot_total // GROUP,)),
        ],
        flops=work,
        moved=8 << 20,
        grant=FORWARD_GRANT,
    )(me, plan, need, values, column, firsts[2], pieces[2])
    partial = call(
        late_kernel,
        pltpu.HBM((n_cols, cap * blk + EXTRA, width), BF16),
        [SMEM, SMEM, VMEM, VMEM, VMEM, VMEM, VMEM, VMEM],
        [
            pltpu.VMEM((row_slots + 1, blk, width), F32),
            pltpu.VMEM((2 * cap * n_y, blk, width), BF16),
            pltpu.VMEM((n_cols, cap * blk + EXTRA, width), BF16),
            pltpu.SemaphoreType.DMA((PARTS,)),
        ],
        flops=work // 2,
        moved=8 << 20,
        out_spec=HBM,
        grant=FORWARD_GRANT,
    )(plan, row_need[0, 0], early, late, firsts[1], pieces[1], firsts[3], pieces[3])
    asked = jnp.concatenate([need, *tables], axis=0)
    bit = 1
    while bit < n_y:
        other = trade(asked, "gr", bit * NX)
        asked = jnp.concatenate([asked, other], axis=0)
        bit *= 2
    partial = swap(partial, "gc")
    activated, back, term = call(
        middle_kernel,
        (
            jax.ShapeDtypeStruct((local, width), BF16),
            pltpu.HBM((n_cols, cap * blk, width), BF16),
            jax.ShapeDtypeStruct((width, width), F32),
        ),
        [VMEM, VMEM, VMEM],
        [pltpu.VMEM((per_dev, blk, width), BF16)],
        flops=work // 8,
        moved=4 << 20,
    )(partial, weight, out_grad[0, 0])
    back = swap(back, "gc")

    halved = [1, 2]
    for bit in halved:
        low, high = jnp.split(term, 2, axis=0)
        top = upper("gr", bit)
        term = jnp.where(top, high, low) + trade(jnp.where(top, low, high), "gr", bit)
    for bit in (4, 8, 16):
        other = trade(term, "gr", bit)
        term = term + other
    bit = 1
    while bit < n_cols:
        term = term + trade(term, "gc", bit)
        bit *= 2
    for bit in reversed(halved):
        other = trade(term, "gr", bit)
        top = upper("gr", bit)
        term = jnp.concatenate([jnp.where(top, other, term), jnp.where(top, term, other)], axis=0)
    node_total = local * n_rows * n_cols
    weight_grad = term * float(node_total) ** (-0.5)

    returned = call(
        functools.partial(backward_kernel, col_slots),
        pltpu.HBM((n_rows, cap * blk, width), BF16),
        [SMEM, SMEM, HBM, VMEM],
        [
            pltpu.VMEM(values.shape, BF16),
            pltpu.VMEM((col_slots, blk, width), F32),
            pltpu.VMEM((n_rows, cap * blk, width), BF16),
            pltpu.SemaphoreType.DMA((slot_total // GROUP,)),
            pltpu.SemaphoreType.DMA((PARTS,)),
        ],
        flops=work,
        moved=8 << 20,
        out_spec=HBM,
        grant=BACKWARD_GRANT,
    )(slots, live_count, values, back.reshape(row_slots, blk, width))
    returned = swap(returned, "gr")
    input_grad = call(
        final_kernel,
        jax.ShapeDtypeStruct((local, width), BF16),
        [SMEM, SMEM, VMEM],
        [pltpu.VMEM((per_dev, blk, width), F32), pltpu.VMEM((per_dev, blk, width), F32)],
        moved=4 << 20,
    )(me, asked, returned)
    return (
        activated.reshape(1, 1, local, width),
        weight_grad,
        input_grad.reshape(1, 1, local, width),
    )


def solution(mesh):
    placed = (
        P("gc", "gr", None, None),
        P("gr", "gc", None, None),
        P(),
        P("gr", "gc", None, None, None),
        P("gr", "gc", None),
        P("gr", "gc"),
        P("gr", "gc", None, None),
        P("gr", "gc", None, None),
    )

    return jax.shard_map(
        on_device,
        mesh=mesh,
        in_specs=placed,
        out_specs=(P("gr", "gc", None, None), P(), P("gc", "gr", None, None)),
        check_vma=False,
    )
```
